512 devices in a mesh: dom: 32 (over z, x), group: 16 (over y, core).
Axes of the slice: x: 4, y: 8, z: 8, core: 2. Of those that a mesh axis runs over, the one named last changes fastest.
Arguments:
- features: bfloat16 [1048576, 256], P(('dom', 'group')), may hold values from -6 to 6
- boundary: int32 [8192], P(('dom', 'group')), may hold values from 0 to 127, as said below
- request: int32 [8192, 6], P(('dom', 'group')), may hold values from 0 to 15, as said below
- tile_slots: int32 [8192, 8], P(('dom', 'group')), may hold values from 0 to 223, as said below
- neighbors: int32 [1048576, 10], P(('dom', 'group')), may hold values from 0 to 127
- negatives: int32 [1048576, 4], P(('dom', 'group')), may hold values from 0 to 127
- layer_weight: bfloat16 [512, 256], replicated, may hold values from -0.25 to 0.25
Outputs:
- feature_grad: float32 [1048576, 256], P(('dom', 'group'))
- weight_grad: float32 [512, 256], replicated
- loss_mean: float32 [], replicated
The draws below stay inside these ranges and needn't reach their ends.
Inputs may be any that keep to these rules, and one draw needn't show every extreme that they name: The 16 entries boundary[i * 16 to i * 16 + 15] are distinct numbers of device i's own row blocks. `request`: row i * 16 + e holds 6 distinct positions in the boundary list of device (i // 16) * 16 + e. `tile_slots`: entries are numbers s as in the first step; the 128 entries of one device are distinct and include every number from 128 to 223.
All inputs are finite; a program needn't handle non-finite values.
Results may differ from the reference program's by a relative error of at most 0.00075.
The reference program's roundings to bfloat16 on the way (of `candidates`, `counts`, `aggregate`, `embed_half`, `dscores`, `dpreact` and `daggregate`) count: a program that leaves them out, or rounds other values in their place, can miss the bound.
Values may be sent and summed in bfloat16 or wider, within the bound.
A program may use at most 64 MiB of HBM per device.

```python
import jax
import jax.numpy as jnp
from jax import lax

D = 256
NODE_DEV = 2048
TILE = 128
BLK = 16
NBT = 8
DEG = 10
NNEG = 4
TILES = 16
NBD = 128
CAND = 128
PEERS = 16
DEVS = 512
NODES = 1048576
CAP = 6
NBND = 16


def draw_boundary(key, part):
    row_keys = jax.random.split(jax.random.fold_in(key, 3), DEVS)
    picked = jax.vmap(lambda single: jax.random.permutation(single, NBD)[:NBND])(row_keys)
    return picked.reshape(-1).astype(jnp.int32)


def draw_request(key, part):
    row_keys = jax.random.split(jax.random.fold_in(key, 5), DEVS * PEERS)
    picked = jax.vmap(lambda single: jax.random.permutation(single, NBND)[:CAP])(row_keys)
    return picked.astype(jnp.int32)


def draw_tile_slots(key, part):
    folded = jax.random.fold_in(key, 7)
    key_noise, key_mix = jax.random.split(folded, 2)
    received_count = PEERS * CAP
    slot_total = NBD + received_count
    priority = jnp.concatenate([jnp.ones((DEVS, NBD), jnp.int32), 2 * jnp.ones((DEVS, received_count), jnp.int32)], axis=1)
    jitter = jax.random.randint(key_noise, (DEVS, slot_total), 0, 1024, dtype=jnp.int32)
    scored = priority * 4194304 + jitter * slot_total + jnp.arange(slot_total, dtype=jnp.int32)[None, :]
    chosen = lax.top_k(scored, TILES * NBT)[1].astype(jnp.int32)
    shuffle = jax.random.split(key_mix, DEVS)
    mixed = jax.vmap(lambda single, chosen_row: jax.random.permutation(single, chosen_row))(shuffle, chosen)
    return mixed.reshape(DEVS * TILES, NBT).astype(jnp.int32)


def plant(result, rng, smallest, top_value):
    longest = result.shape.index(max(result.shape))
    spots = []
    for shift in (0, 1):
        where = [jax.random.randint(jax.random.fold_in(rng, axis), (), 0, length) for axis, length in enumerate(result.shape)]
        where[longest] = (where[longest] + shift) % result.shape[longest]
        spots.append(tuple(where))
    return result.at[spots[0]].set(smallest).at[spots[1]].set(top_value)


def levels(stream_key, extent, shards, smallest, largest):
    def one(dim, blocks):
        heights = jax.random.uniform(jax.random.fold_in(jax.random.fold_in(stream_key, 6), dim), (blocks,), jnp.float32, smallest / len(shards), largest / len(shards))
        return jnp.repeat(jnp.exp(heights), extent[dim] // blocks).reshape((-1,) + (1,) * (len(extent) - dim - 1))

    loudness = one(*shards[0])
    for cut in shards[1:]:
        loudness = loudness * one(*cut)
    return loudness


def gaussian(stream_key, extent, scale, reach, cuts=(), held_as=jnp.bfloat16):
    factor_of = levels(stream_key, extent, cuts, -0.22, 0.18) if cuts else 1.0
    entries = jax.random.normal(stream_key, extent, jnp.float32) * scale * factor_of
    return jnp.minimum(jnp.maximum(entries, -reach), reach).astype(held_as)


def setup_inputs(seed: int = 0) -> dict:
    streams_of = jax.random.split(jax.random.key(seed), 8)
    features = gaussian(streams_of[0], (NODES, D), 1.0, 6.0, ((0, 512),))
    boundary = draw_boundary(jax.random.fold_in(streams_of[7], 71), 0)
    request = draw_request(jax.random.fold_in(streams_of[7], 71), 0)
    tile_slots = draw_tile_slots(jax.random.fold_in(streams_of[7], 71), 0)
    neighbors = plant(jax.random.randint(streams_of[4], (NODES, DEG), 0, CAND), jax.random.fold_in(streams_of[4], 1), 0, CAND - 1).astype(jnp.int32)
    negatives = plant(jax.random.randint(streams_of[5], (NODES, NNEG), 0, CAND), jax.random.fold_in(streams_of[5], 1), 0, CAND - 1).astype(jnp.int32)
    layer_weight = gaussian(streams_of[6], (2 * D, D), (2 * D) ** -0.5, 0.25)
    return {"features": features, "boundary": boundary, "request": request, "tile_slots": tile_slots, "neighbors": neighbors, "negatives": negatives, "layer_weight": layer_weight}


margin = 0.5
epsilon = 1e-06

def contract(form, left, right):
    return jnp.einsum(form, left.astype(jnp.float32), right.astype(jnp.float32))

def tile_terms(own_rows, candidates, neighbor_ids, negative_ids, layer_weight):
    tile_count, tile_rows, feature_width = own_rows.shape
    cand_count = candidates.shape[1]
    degree = neighbor_ids.shape[-1]
    negative_count = negative_ids.shape[-1]
    slot_ids = jnp.arange(cand_count, dtype=jnp.int32)
    counts = lax.optimization_barrier(jnp.sum((neighbor_ids[..., None] == slot_ids).astype(jnp.float32), axis=2)).astype(jnp.bfloat16)
    aggregate = (contract('tuc,tcd->tud', counts, candidates) / degree).astype(jnp.bfloat16)
    joined = jnp.concatenate([own_rows, aggregate], axis=-1).reshape(-1, 2 * feature_width)
    preact = jnp.dot(joined, layer_weight, preferred_element_type=jnp.float32)
    gate_value = jax.nn.sigmoid(preact)
    hidden = preact * gate_value
    norm_scale = lax.rsqrt(lax.optimization_barrier(jnp.mean(hidden * hidden, axis=-1, keepdims=True)) + epsilon)
    embedding = hidden * norm_scale
    embed_half = embedding.astype(jnp.bfloat16).reshape(tile_count, tile_rows, feature_width)
    inv_root = feature_width ** (-0.5)
    scores = contract('tud,tcd->tuc', embed_half, candidates) * inv_root
    positive = (neighbor_ids[..., 0:1] == slot_ids).astype(jnp.float32)
    negative = (negative_ids[..., None] == slot_ids).astype(jnp.float32)
    pos_score = lax.optimization_barrier(jnp.sum(scores * positive, axis=-1, keepdims=True))
    neg_score = lax.optimization_barrier(jnp.sum(scores[:, :, None, :] * negative, axis=-1))
    excess = margin + neg_score - pos_score
    loss_sum = jnp.sum(jax.nn.softplus(excess)) / negative_count
    neg_weight = jax.nn.sigmoid(excess) / negative_count
    dscores = (lax.optimization_barrier(jnp.sum(neg_weight[..., None] * negative, axis=2)) - lax.optimization_barrier(jnp.sum(neg_weight, axis=-1, keepdims=True)) * positive) * inv_root
    dscores_half = dscores.astype(jnp.bfloat16)
    dembedding = contract('tuc,tcd->tud', dscores_half, candidates).reshape(-1, feature_width)
    dcandidates = contract('tuc,tud->tcd', dscores_half, embed_half)
    dhidden = norm_scale * (dembedding - embedding * lax.optimization_barrier(jnp.mean(dembedding * embedding, axis=-1, keepdims=True)))
    dpreact = (dhidden * gate_value * (1.0 + preact * (1.0 - gate_value))).astype(jnp.bfloat16)
    dweight = jnp.dot(joined.T, dpreact, preferred_element_type=jnp.float32)
    dinputs = jnp.dot(dpreact, layer_weight.T, preferred_element_type=jnp.float32)
    dself = dinputs[:, :feature_width].reshape(tile_count, tile_rows, feature_width)
    daggregate = (dinputs[:, feature_width:] / degree).astype(jnp.bfloat16).reshape(tile_count, tile_rows, feature_width)
    dcandidates = dcandidates + contract('tuc,tud->tcd', counts, daggregate)
    return (loss_sum, dweight, dself, dcandidates)

def reference(features, boundary, request, tile_slots, neighbors, negatives, layer_weight):
    all_blocks = features.reshape(-1, BLK, D)

    def device_step(carried, device):
        gradients, dweight_sum, loss_total = carried
        slot_list = lax.dynamic_slice_in_dim(tile_slots, device * TILES, TILES).reshape(-1)
        wanted = lax.dynamic_slice_in_dim(request, device * PEERS, PEERS).reshape(-1)
        received_slot = jnp.clip(slot_list - NBD, 0, PEERS * CAP - 1)
        peer_index = received_slot // CAP
        owner_device = device // PEERS * PEERS + peer_index
        position = wanted[received_slot]
        local_block = boundary[owner_device * NBND + position]
        remote = owner_device * NBD + local_block
        block_ids = jnp.where(slot_list < NBD, device * NBD + slot_list, remote).astype(jnp.int32)
        candidates = all_blocks[block_ids].reshape(TILES, CAND, D)
        own_rows = lax.dynamic_slice_in_dim(features, device * NODE_DEV, NODE_DEV).reshape(TILES, TILE, D)
        neighbor_ids = lax.dynamic_slice_in_dim(neighbors, device * NODE_DEV, NODE_DEV).reshape(TILES, TILE, DEG)
        negative_ids = lax.dynamic_slice_in_dim(negatives, device * NODE_DEV, NODE_DEV).reshape(TILES, TILE, NNEG)
        loss_sum, dweight, dself, dcandidates = tile_terms(own_rows, candidates, neighbor_ids, negative_ids, layer_weight)
        current = lax.dynamic_slice_in_dim(gradients, device * NBD, NBD)
        gradients = lax.dynamic_update_slice_in_dim(gradients, current + dself.reshape(NBD, BLK, D), device * NBD, 0)
        gradients = gradients.at[block_ids].add(dcandidates.reshape(-1, BLK, D))
        return ((gradients, dweight_sum + dweight, loss_total + loss_sum), None)
    start = (jnp.zeros((DEVS * NBD, BLK, D), jnp.float32), jnp.zeros((2 * D, D), jnp.float32), jnp.zeros((), jnp.float32))
    finished, _ = lax.scan(device_step, start, jnp.arange(DEVS, dtype=jnp.int32))
    gradients, dweight_sum, loss_total = finished
    return (gradients.reshape(-1, D), dweight_sum / NODE_DEV, loss_total / NODES)
```

```python
import functools

import jax
import jax.numpy as jnp
from jax import lax
from jax.experimental import pallas as pl
from jax.experimental.pallas import tpu as pltpu
from jax.sharding import Mesh
from jax.sharding import PartitionSpec as P

MESH = pl.DeviceIdType.MESH
TILE = 128
BLK = 16
NBT = 8
DEG = 10
NNEG = 4
CAP = 6
TILES = 16
NODES = 2048
D = 256
NBD = 128
NBND = 16
ROWS = NBND * BLK
PEERS = 16
TABLE = NODES + PEERS * ROWS
NY = 8
NZ = 8
NX = 4
f32 = jnp.float32
bf16 = jnp.bfloat16
AXES = ("z", "x", "y", "c")


def place():
    return tuple(lax.axis_index(a) for a in AXES)


def remote(src, dst, send, recv, device):
    return pltpu.make_async_remote_copy(
        src_ref=src, dst_ref=dst, send_sem=send, recv_sem=recv, device_id=device, device_id_type=MESH
    )


SUBS = 4
SUB = ROWS // SUBS


def gather_kernel(boundary, feat, out, buf, rs, rr, ls, lr, cs, cr, outs):
    z, x, y, c = place()
    right = (z, x, lax.rem(y + 1, NY), c)
    left = (z, x, lax.rem(y + NY - 1, NY), c)
    mate = (z, x, y, 1 - c)

    def slot(yy, cc):
        return lax.rem(yy + NY, NY) * 2 + cc

    me = slot(y, c)
    for p in range(NBND):
        buf[me, pl.ds(p * BLK, BLK), :] = feat[boundary[p]]
    barrier = pltpu.get_barrier_semaphore()
    for d in (right, left, mate):
        pl.semaphore_signal(barrier, inc=1, device_id=d, device_id_type=MESH)
    pl.semaphore_wait(barrier, 3)

    def piece(s, q):
        return buf.at[s, pl.ds(q * SUB, SUB), :]

    def to_right(d, q):
        v = piece(slot(y - d, c), q)
        return remote(v, v, rs.at[d, q], rr.at[d, q], right)

    def from_left(d, q):
        v = piece(slot(y - 1 - d, c), q)
        return remote(v, v, rs.at[d, q], rr.at[d, q], right)

    def to_left(d, q):
        v = piece(slot(y + d, c), q)
        return remote(v, v, ls.at[d, q], lr.at[d, q], left)

    def from_right(d, q):
        v = piece(slot(y + 1 + d, c), q)
        return remote(v, v, ls.at[d, q], lr.at[d, q], left)

    def to_mate(k, s, q):
        v = piece(s, q)
        return remote(v, v, cs.at[k, q], cr.at[k, q], mate)

    def from_mate(k, s, q):
        v = piece(s, q)
        return remote(v, v, cs.at[k, q], cr.at[k, q], mate)

    half = SUBS // 2
    sent = []

    def go(copy):
        copy.start()
        sent.append(copy)

    for q in range(SUBS):
        go(to_right(0, q))
        go(to_left(0, SUBS - 1 - q))
    for q in range(SUBS):
        go(to_mate(0, me, q))
    for d in range(1, 5):
        for q in range(SUBS):
            if d < 4 or q < half:
                from_left(d - 1, q).wait_recv()
                if d < 3 or (d == 3 and q < half):
                    go(to_right(d, q))
                go(to_mate(d, slot(y - d, c), q))
            b = SUBS - 1 - q
            if d < 4 or b >= half:
                from_right(d - 1, b).wait_recv()
                if d < 3 or (d == 3 and b >= half):
                    go(to_left(d, b))
                go(to_mate(d if d == 4 else 8 - d, slot(y + d, c), b))
    o = 1 - c
    for k in range(8):
        for q in range(SUBS):
            from_mate(k, slot(y - k, o), q).wait_recv()
    copy = pltpu.make_async_copy(buf, out, outs)
    copy.start()
    for s in sent:
        s.wait_send()
    copy.wait()


def gathered(boundary, features):
    sem = pltpu.SemaphoreType.DMA
    return pl.pallas_call(
        gather_kernel,
        out_shape=jax.ShapeDtypeStruct((PEERS, ROWS, D), bf16),
        in_specs=[pl.BlockSpec(memory_space=pltpu.SMEM), pl.BlockSpec(memory_space=pltpu.VMEM)],
        out_specs=pl.BlockSpec(memory_space=pl.ANY),
        scratch_shapes=[
            pltpu.VMEM((PEERS, ROWS, D), bf16),
            sem((4, SUBS)),
            sem((4, SUBS)),
            sem((4, SUBS)),
            sem((4, SUBS)),
            sem((8, SUBS)),
            sem((8, SUBS)),
            sem(()),
        ],
        compiler_params=pltpu.CompilerParams(collective_id=0, has_side_effects=True),
        name="boundary_gather",
    )(boundary, features)


def over(a, b, da, db):
    return lax.dot_general(a, b, (((da,), (db,)), ((), ())), preferred_element_type=f32)


def layer_kernel(
    slots, req, nbr, neg, weight, feat_hbm, far_hbm,
    own_out, far_out, dw_out, loss_out,
    table, grads, aggs, dpres, sems,
):
    c1 = pltpu.make_async_copy(feat_hbm, table.at[pl.ds(0, NODES), :], sems.at[0])
    c2 = pltpu.make_async_copy(far_hbm, table.at[pl.ds(NODES, PEERS * ROWS), :], sems.at[1])
    c1.start()
    c2.start()

    @pl.loop(0, TABLE // 256)
    def _(i):
        grads[pl.ds(pl.multiple_of(i * 256, 256), 256), :] = jnp.zeros((256, D), f32)

    c1.wait()
    c2.wait()
    kio = lax.broadcasted_iota(jnp.int32, (TILE, TILE), 0)
    inv_root = D ** (-0.5)

    def tile(t, loss):
        base = pl.multiple_of(t * TILE, TILE)
        rows = []
        for j in range(NBT):
            s = slots[j, t]
            n = jnp.maximum(s - NBD, 0)
            e = (n * 43) >> 8
            b = jnp.where(s < NBD, s, NBD + e * NBND + req[n - e * CAP, e])
            rows.append(pl.multiple_of(b * BLK, BLK))
        cand = jnp.concatenate([table[pl.ds(r, BLK), :] for r in rows], axis=0)
        nb = nbr[:, pl.ds(base, TILE)]
        ng = neg[:, pl.ds(base, TILE)]
        counts = jnp.zeros((TILE, TILE), f32)
        for j in range(DEG):
            counts += jnp.where(nb[j : j + 1, :] == kio, 1.0, 0.0)
        counts = counts.astype(bf16)
        x = table[pl.ds(base, TILE), :]
        agg = (over(counts, cand, 0, 0) / DEG).astype(bf16)
        pre = over(x, weight[:D, :], 1, 0) + over(agg, weight[D:, :], 1, 0)
        gate = jax.nn.sigmoid(pre)
        hid = pre * gate
        scale = lax.rsqrt(jnp.mean(hid * hid, axis=-1, keepdims=True) + 1e-06)
        emb = hid * scale
        eh = emb.astype(bf16)
        sc = over(cand, eh, 1, 1) * inv_root
        pos = nb[0:1, :] == kio
        ps = jnp.sum(jnp.where(pos, sc, 0.0), axis=0, keepdims=True)
        negs = [ng[n : n + 1, :] == kio for n in range(NNEG)]
        ns = [jnp.sum(jnp.where(m, sc, 0.0), axis=0, keepdims=True) for m in negs]
        ex = 0.5 + jnp.concatenate(ns, axis=0) - ps
        loss += jax.nn.softplus(ex) * 0.25
        w = jax.nn.sigmoid(ex) * 0.25
        wsum = jnp.sum(w, axis=0, keepdims=True)
        ds = jnp.where(negs[0], w[0:1, :], 0.0)
        for n in range(1, NNEG):
            ds += jnp.where(negs[n], w[n : n + 1, :], 0.0)
        ds = (ds - jnp.where(pos, wsum, 0.0)) * inv_root
        ds = ds.astype(bf16)
        demb = over(ds, cand, 0, 0)
        m2 = jnp.mean(demb * emb, axis=-1, keepdims=True)
        dh = scale * (demb - emb * m2)
        dpre = (dh * gate * (1.0 + pre * (1.0 - gate))).astype(bf16)
        aggs[pl.ds(base, TILE), :] = agg
        dpres[pl.ds(base, TILE), :] = dpre
        dself = over(dpre, weight[:D, :], 1, 1)
        dagg = (over(dpre, weight[D:, :], 1, 1) / DEG).astype(bf16)
        dc = over(ds, eh, 1, 0) + over(counts, dagg, 1, 0)
        grads[pl.ds(base, TILE), :] += dself
        for j in range(NBT):
            grads[pl.ds(rows[j], BLK), :] += dc[j * BLK : (j + 1) * BLK, :]
        return loss

    loss = lax.fori_loop(0, TILES, tile, jnp.zeros((NNEG, TILE), f32))
    o1 = pltpu.make_async_copy(grads.at[pl.ds(NODES, PEERS * ROWS), :], far_out, sems.at[2])
    o2 = pltpu.make_async_copy(grads.at[pl.ds(0, NODES), :], own_out, sems.at[3])
    o1.start()
    o2.start()
    dp = dpres[...]
    for h in range(2):
        src = table[pl.ds(0, NODES), :] if h == 0 else aggs[...]
        dw = over(src, dp, 0, 0)
        for l in range(2):
            dw_out[l * 512 + h * 256 : l * 512 + h * 256 + 256, :] = dw[:, l * 128 : l * 128 + 128]
    loss_out[...] = jnp.broadcast_to(jnp.sum(loss, keepdims=True), (8, 128))
    o1.wait()
    o2.wait()


def layer(slots, req, nbr, neg, weight, features, far):
    vm = pl.BlockSpec(memory_space=pltpu.VMEM)
    sm = pl.BlockSpec(memory_space=pltpu.SMEM)
    hbm = pl.BlockSpec(memory_space=pl.ANY)
    return pl.pallas_call(
        layer_kernel,
        out_shape=(
            jax.ShapeDtypeStruct((NODES, D), f32),
            jax.ShapeDtypeStruct((PEERS * ROWS, D), f32),
            jax.ShapeDtypeStruct((1024, 128), f32),
            jax.ShapeDtypeStruct((8, 128), f32),
        ),
        in_specs=[sm, sm, vm, vm, vm, hbm, hbm],
        out_specs=(hbm, hbm, vm, vm),
        scratch_shapes=[
            pltpu.VMEM((TABLE, D), bf16),
            pltpu.VMEM((TABLE, D), f32),
            pltpu.VMEM((NODES, D), bf16),
            pltpu.VMEM((NODES, D), bf16),
            pltpu.SemaphoreType.DMA((4,)),
        ],
        name="layer",
    )(slots, req, nbr, neg, weight, features, far)


HALF = ROWS // 2


def reduce_kernel(
    part, dw, lossp, out, dw_out, loss_out,
    mine, mates, rbuf, lbuf, rsend, lsend,
    w0, sum0, lossb, a1, b1, a2, b2, sum1, sum3, sum2, ybuf, total, ag2a, ag2b, ag1,
    ms, mr, lsem, rs, rr, ls, lr, ws, wr,
):
    z, x, y, c = place()
    o = 1 - c
    right = (z, x, lax.rem(y + 1, NY), c)
    left = (z, x, lax.rem(y + NY - 1, NY), c)
    mate = (z, x, y, o)

    def zs(k):
        return (lax.rem(z + k, NZ), x, y, c)

    def xs(k):
        return (z, lax.rem(x + k, NX), y, c)

    def ys(k):
        return (z, x, lax.rem(y + k, NY), c)

    peers = [mate] + [zs(k) for k in range(1, NZ)] + [xs(k) for k in range(1, NX)] + [ys(k) for k in range(1, NY)]
    barrier = pltpu.get_barrier_semaphore()
    for d in peers:
        pl.semaphore_signal(barrier, inc=1, device_id=d, device_id_type=MESH)
    pl.semaphore_wait(barrier, len(peers))

    sent = []

    def go(copy):
        copy.start()
        sent.append(copy)
        return copy

    def rows(first, n):
        return pl.ds(pl.multiple_of(first, 8), n)

    first = [
        remote(dw.at[rows(o * 512, 512), :], w0, ws.at[0, 0], wr.at[0, 0], mate),
        remote(lossp, lossb.at[0], ws.at[0, 1], wr.at[0, 1], mate),
    ]
    for copy in first:
        go(copy)

    def owner(k):
        return lax.rem(y + k + NY, NY)

    order = [4, 3, -3, 2, -2, 1, -1, 0]
    mcopies = {}
    for i, k in enumerate(order):
        oo = owner(k)
        lc = pltpu.make_async_copy(part.at[rows((oo * 2 + c) * ROWS, ROWS), :], mine.at[i], lsem.at[i])
        lc.start()
        rc = go(remote(part.at[rows((oo * 2 + o) * ROWS, ROWS), :], mates.at[i], ms.at[i], mr.at[i], mate))
        mcopies[k] = (lc, rc)
    ready = {}

    def pair(k, h):
        if k not in ready:
            lc, rc = mcopies[k]
            lc.wait()
            rc.wait_recv()
            ready[k] = True
        i = order.index(k)
        return mine[i, h * HALF : (h + 1) * HALF, :] + mates[i, h * HALF : (h + 1) * HALF, :]

    def hop(to_right, s, h):
        sb, rb, ss, rsm, dev = (rsend, rbuf, rs, rr, right) if to_right else (lsend, lbuf, ls, lr, left)
        view = pl.ds(h * HALF, HALF)
        return remote(sb.at[s, view, :], rb.at[s, view, :], ss.at[s, h], rsm.at[s, h], dev)

    def ring(to_right, s, h):
        start = 0 if (h == 0) == to_right else 1
        if s < start:
            return
        k = 4 - s if to_right else (-(4 - s) if s else 4)
        v = pair(k, h)
        if s > start:
            hop(to_right, s - 1, h).wait_recv()
            v = v + (rbuf if to_right else lbuf)[s - 1, h * HALF : (h + 1) * HALF, :]
        (rsend if to_right else lsend)[s, h * HALF : (h + 1) * HALF, :] = v
        go(hop(to_right, s, h))

    def r0():
        ring(True, 0, 0)
        ring(False, 0, 1)

    def r1a():
        ring(True, 1, 1)
        ring(False, 1, 0)

    def r1b():
        ring(True, 1, 0)
        ring(False, 1, 1)

    def r2a():
        ring(True, 2, 1)
        ring(False, 2, 0)

    def r2b():
        ring(True, 2, 0)
        ring(False, 2, 1)

    def r3a():
        ring(True, 3, 1)
        ring(False, 3, 0)

    def r3b():
        ring(True, 3, 0)
        ring(False, 3, 1)

    def r4():
        for h in (1, 0):
            v = pair(0, h)
            hop(True, 3, h).wait_recv()
            hop(False, 3, h).wait_recv()
            view = slice(h * HALF, (h + 1) * HALF)
            out[view, :] = v + rbuf[3, view, :] + lbuf[3, view, :]

    def scatter(stage, src, base, r, buf, n, me, dev):
        buf[me] = src[rows(base + me * r, r), :]
        for k in range(1, n):
            to = lax.rem(me + k, n)
            go(remote(src.at[rows(base + to * r, r), :], buf.at[me], ws.at[stage, k], wr.at[stage, me], dev(k)))

    def arrived(stage, buf, n, me, dev):
        for k in range(1, n):
            who = lax.rem(me + k, n)
            remote(buf.at[who], buf.at[who], ws.at[stage, k], wr.at[stage, who], dev(k)).wait_recv()

    def spread(stage, src, buf, n, me, dev):
        buf[me] = src[...]
        for k in range(1, n):
            go(remote(src, buf.at[me], ws.at[stage, k], wr.at[stage, me], dev(k)))

    def summed(buf, n):
        v = buf[0]
        for i in range(1, n):
            v = v + buf[i]
        return v

    lz, lx, lossz, lossx = lossb.at[pl.ds(2, NZ)], lossb.at[pl.ds(10, NX)], lossb.at[14], lossb.at[15]

    def wa():
        for copy in first:
            copy.wait_recv()
        sum0[...] = dw[rows(c * 512, 512), :] + w0[...]
        lossb[1] = lossp[...] + lossb[0]
        scatter(1, sum0, 0, 32, a1, NZ, z, zs)
        scatter(2, sum0, 256, 64, b1, NX, x, xs)
        spread(3, lossb.at[1], lz, NZ, z, zs)

    def wb():
        arrived(2, b1, NX, x, xs)
        sum1[32:96, :] = summed(b1, NX)
        scatter(4, sum1, 32, 8, b2, NZ, z, zs)

    def wc():
        arrived(1, a1, NZ, z, zs)
        arrived(3, lz, NZ, z, zs)
        sum1[0:32, :] = summed(a1, NZ)
        lossb[14] = summed(lz, NZ)
        scatter(5, sum1, 0, 8, a2, NX, x, xs)
        spread(6, lossz, lx, NX, x, xs)

    def wd():
        arrived(4, b2, NZ, z, zs)
        arrived(5, a2, NX, x, xs)
        arrived(6, lx, NX, x, xs)
        sum2[0:8, :] = summed(a2, NX)
        sum2[8:16, :] = summed(b2, NZ)
        sum2[16:24, :] = summed(lx, NX)
        spread(7, sum2, ybuf, NY, y, ys)

    def we():
        arrived(7, ybuf, NY, y, ys)
        t = summed(ybuf, NY)
        total[...] = t
        loss_out[...] = t[16:24, :]
        spread(8, total.at[pl.ds(0, 8), :], ag2a, NX, x, xs)
        spread(9, total.at[pl.ds(8, 8), :], ag2b, NZ, z, zs)

    def wide(stage, src, r, base, n, me, dev):
        for k in range(1, n):
            go(remote(src, ag1.at[rows(base + me * r, r), :], ws.at[stage, k], wr.at[stage, me], dev(k)))

    def wide_arrived(stage, r, base, n, me, dev):
        for k in range(1, n):
            who = lax.rem(me + k, n)
            v = ag1.at[rows(base + who * r, r), :]
            remote(v, v, ws.at[stage, k], wr.at[stage, who], dev(k)).wait_recv()

    def wf():
        arrived(8, ag2a, NX, x, xs)
        for i in range(NX):
            sum3[i * 8 : i * 8 + 8, :] = ag2a[i]
        wide(10, sum3.at[pl.ds(0, 32), :], 32, 0, NZ, z, zs)
        ag1[rows(z * 32, 32), :] = sum3[0:32, :]

    def wg():
        arrived(9, ag2b, NZ, z, zs)
        for i in range(NZ):
            sum3[32 + i * 8 : 40 + i * 8, :] = ag2b[i]
        wide(11, sum3.at[pl.ds(32, 64), :], 64, 256, NX, x, xs)
        ag1[rows(256 + x * 64, 64), :] = sum3[32:96, :]

    last = []

    def wh():
        wide_arrived(11, 64, 256, NX, x, xs)
        last.append(go(remote(ag1.at[pl.ds(256, 256), :], dw_out.at[rows(c * 512 + 256, 256), :], ws.at[12, 1], wr.at[12, 1], mate)))
        dw_out[rows(c * 512 + 256, 256), :] = ag1[256:512, :]

    def wi():
        wide_arrived(10, 32, 0, NZ, z, zs)
        last.append(go(remote(ag1.at[pl.ds(0, 256), :], dw_out.at[rows(c * 512, 256), :], ws.at[12, 0], wr.at[12, 0], mate)))
        dw_out[rows(c * 512, 256), :] = ag1[0:256, :]
        for copy in last:
            copy.wait_recv()

    for step in (wa, r0, r1a, wb, r1b, r2a, wc, wd, r2b, we, r3a, wg, wf, r3b, wh, r4, wi):
        step()
    for copy in sent:
        copy.wait_send()


def reduced(part, dw, lossp):
    vm = pl.BlockSpec(memory_space=pltpu.VMEM)
    hbm = pl.BlockSpec(memory_space=pl.ANY)
    sem = pltpu.SemaphoreType.DMA
    V = pltpu.VMEM
    return pl.pallas_call(
        reduce_kernel,
        out_shape=(
            jax.ShapeDtypeStruct((ROWS, D), f32),
            jax.ShapeDtypeStruct((1024, 128), f32),
            jax.ShapeDtypeStruct((8, 128), f32),
        ),
        in_specs=[hbm, vm, vm],
        out_specs=(vm, vm, vm),
        scratch_shapes=[
            V((8, ROWS, D), f32),
            V((8, ROWS, D), f32),
            V((4, ROWS, D), f32),
            V((4, ROWS, D), f32),
            V((4, ROWS, D), f32),
            V((4, ROWS, D), f32),
            V((512, 128), f32),
            V((512, 128), f32),
            V((16, 8, 128), f32),
            V((NZ, 32, 128), f32),
            V((NX, 64, 128), f32),
            V((NX, 8, 128), f32),
            V((NZ, 8, 128), f32),
            V((96, 128), f32),
            V((96, 128), f32),
            V((24, 128), f32),
            V((NY, 24, 128), f32),
            V((24, 128), f32),
            V((NX, 8, 128), f32),
            V((NZ, 8, 128), f32),
            V((512, 128), f32),
            sem((8,)),
            sem((8,)),
            sem((8,)),
            sem((4, 2)),
            sem((4, 2)),
            sem((4, 2)),
            sem((4, 2)),
            sem((13, 8)),
            sem((13, 8)),
        ],
        compiler_params=pltpu.CompilerParams(collective_id=1, has_side_effects=True),
        name="sums",
    )(part, dw, lossp)


def add_kernel(boundary, got, own, out, buf, rsem, wsem):
    for p in range(NBND):
        row = pl.multiple_of(boundary[p] * BLK, BLK)
        pltpu.make_async_copy(own.at[pl.ds(row, BLK), :], buf.at[pl.ds(p * BLK, BLK), :], rsem.at[p]).start()
    for p in range(NBND):
        row = pl.multiple_of(boundary[p] * BLK, BLK)
        view = pl.ds(p * BLK, BLK)
        pltpu.make_async_copy(own.at[pl.ds(row, BLK), :], buf.at[view, :], rsem.at[p]).wait()
        buf[view, :] += got[view, :]
        pltpu.make_async_copy(buf.at[view, :], out.at[pl.ds(row, BLK), :], wsem.at[p]).start()
    for p in range(NBND):
        row = pl.multiple_of(boundary[p] * BLK, BLK)
        pltpu.make_async_copy(buf.at[pl.ds(p * BLK, BLK), :], out.at[pl.ds(row, BLK), :], wsem.at[p]).wait()


def added(boundary, got, own):
    hbm = pl.BlockSpec(memory_space=pl.ANY)
    return pl.pallas_call(
        add_kernel,
        out_shape=jax.ShapeDtypeStruct((NODES, D), f32),
        in_specs=[pl.BlockSpec(memory_space=pltpu.SMEM), pl.BlockSpec(memory_space=pltpu.VMEM), hbm],
        out_specs=hbm,
        scratch_shapes=[
            pltpu.VMEM((ROWS, D), f32),
            pltpu.SemaphoreType.DMA((NBND,)),
            pltpu.SemaphoreType.DMA((NBND,)),
        ],
        input_output_aliases={2: 0},
        name="add_returned",
    )(boundary, got, own)


def per_device(features, boundary, request, tile_slots, neighbors, negatives, layer_weight):
    far = gathered(boundary, features.reshape(NBD, BLK, D))
    own, part, dw, lossp = layer(
        tile_slots.T, request.T, neighbors.T, negatives.T, layer_weight, features, far.reshape(PEERS * ROWS, D)
    )
    got, dwt, losst = reduced(part, dw, lossp)
    grad = added(boundary, got, own)
    wgrad = jnp.concatenate([dwt[:512], dwt[512:]], axis=1) / NODES
    return grad, wgrad, losst[0, 0] / (NODES * 512)


def solution(mesh):
    finer = Mesh(mesh.devices.reshape(NZ, NX, NY, 2), AXES)
    dg = AXES
    return jax.shard_map(
        per_device,
        mesh=finer,
        in_specs=(P(dg, None), P(dg), P(dg, None), P(dg, None), P(dg, None), P(dg, None), P()),
        out_specs=(P(dg, None), P(), P()),
        check_vma=False,
    )
```

```python
import functools

import jax
import jax.numpy as jnp
from jax import lax
from jax.experimental import pallas as pl
from jax.experimental.pallas import tpu as pltpu
from jax.sharding import Mesh
from jax.sharding import PartitionSpec as P

MESH = pl.DeviceIdType.MESH
TILE = 128
BLK = 16
NBT = 8
DEG = 10
NNEG = 4
CAP = 6
TILES = 16
NODES = 2048
D = 256
NBD = 128
NBND = 16
ROWS = NBND * BLK
PEERS = 16
TABLE = NODES + PEERS * ROWS
NY = 8
NZ = 8
NX = 4
f32 = jnp.float32
bf16 = jnp.bfloat16
AXES = ("z", "x", "y", "c")


def place():
    return tuple(lax.axis_index(a) for a in AXES)


def remote(src, dst, send, recv, device):
    return pltpu.make_async_remote_copy(
        src_ref=src, dst_ref=dst, send_sem=send, recv_sem=recv, device_id=device, device_id_type=MESH
    )


SUBS = 4
SUB = NBND // SUBS
HALF = NBND // 2
GROUP = 4


def over(a, b, da, db):
    return lax.dot_general(a, b, (((da,), (db,)), ((), ())), preferred_element_type=f32)


def index_kernel(slots, req, out):
    @pl.loop(0, 48)
    def _(i):
        for j in range(8):
            out[NBD + i * 8 + j] = NBD

    @pl.loop(0, TILES)
    def _(t):
        for j in range(NBT):
            s = slots[j, t]
            n = jnp.maximum(s - NBD, 0)
            e = (n * 43) >> 8
            b = jnp.where(s < NBD, s, NBD + e * NBND + req[n - e * CAP, e])
            out[t * NBT + j] = b
            out[NBD + b] = t * NBT + j


def indices(slots, req):
    sm = pl.BlockSpec(memory_space=pltpu.SMEM)
    return pl.pallas_call(
        index_kernel,
        out_shape=jax.ShapeDtypeStruct((512,), jnp.int32),
        in_specs=[sm, sm],
        out_specs=sm,
        name="indices",
    )(slots, req)


def layer_kernel(
    places, boundary, nbr, neg, weight, feat,
    own_out, out, dw_out, loss_out,
    table, cand, ct, cn, xw, aggs, emb, slope, eh, dss, dpres, own, cg, pre,
    msend, mates, rbuf, lbuf, rsend, lsend,
    dw, lossp, w0, sum0, lossb, a1, b1, a2, b2, sum1, sum3, sum2, ybuf, total, ag2a, ag2b, ag1,
    fsem, osem, grs, grr, gls, glr, gcs, gcr, ms, mr, rs, rr, ls, lr, ws, wr,
):
    z, x, y, c = place()
    o = 1 - c
    right = (z, x, lax.rem(y + 1, NY), c)
    left = (z, x, lax.rem(y + NY - 1, NY), c)
    mate = (z, x, y, o)

    def zs(k):
        return (lax.rem(z + k, NZ), x, y, c)

    def xs(k):
        return (z, lax.rem(x + k, NX), y, c)

    def ys(k):
        return (z, x, lax.rem(y + k, NY), c)

    sent = []

    def go(copy):
        copy.start()
        sent.append(copy)
        return copy

    def rows(first, n):
        return pl.ds(pl.multiple_of(first, 8), n)

    def slot(yy, cc):
        return NBD + (lax.rem(yy + NY, NY) * 2 + cc) * NBND

    load = pltpu.make_async_copy(feat, table.at[pl.ds(0, NBD)], fsem)
    load.start()
    load.wait()
    me = slot(y, c)
    for p in range(NBND):
        table[me + p] = table[boundary[p]]
    peers = [mate] + [zs(k) for k in range(1, NZ)] + [xs(k) for k in range(1, NX)] + [ys(k) for k in range(1, NY)]
    barrier = pltpu.get_barrier_semaphore()
    for d in peers:
        pl.semaphore_signal(barrier, inc=1, device_id=d, device_id_type=MESH)

    kio = lax.broadcasted_iota(jnp.int32, (TILE, TILE), 0)
    inv_root = D ** (-0.5)

    def at(t, n=1):
        return pl.ds(pl.multiple_of(t * TILE, TILE), n * TILE)

    def counted(g, _):
        for i in range(2):
            t = g * 2 + i
            nb = nbr[:, at(t)]
            v = jnp.zeros((TILE, TILE), f32)
            for j in range(DEG):
                v += jnp.where(nb[j : j + 1, :] == kio, 1.0, 0.0)
            ct[at(t), :] = v.astype(bf16)
            cn[at(t), :] = v.T.astype(bf16)
        return 0

    lax.fori_loop(0, TILES // 2, counted, 0)
    pl.semaphore_wait(barrier, len(peers))

    def piece(s, q):
        return table.at[pl.ds(s + q * SUB, SUB)]

    def to_right(d, q):
        v = piece(slot(y - d, c), q)
        return remote(v, v, grs.at[d, q], grr.at[d, q], right)

    def from_left(d, q):
        v = piece(slot(y - 1 - d, c), q)
        return remote(v, v, grs.at[d, q], grr.at[d, q], right)

    def to_left(d, q):
        v = piece(slot(y + d, c), q)
        return remote(v, v, gls.at[d, q], glr.at[d, q], left)

    def from_right(d, q):
        v = piece(slot(y + 1 + d, c), q)
        return remote(v, v, gls.at[d, q], glr.at[d, q], left)

    def mate_copy(k, s, q):
        v = piece(s, q)
        return remote(v, v, gcs.at[k, q], gcr.at[k, q], mate)

    half = SUBS // 2
    for q in range(SUBS):
        go(to_right(0, q))
        go(to_left(0, SUBS - 1 - q))
    for q in range(SUBS):
        go(mate_copy(0, me, q))

    def own_part(g):
        v = table[pl.ds(g * GROUP * NBT, GROUP * NBT)].reshape(GROUP * TILE, D)
        xw[at(g * GROUP, GROUP), :] = over(v, weight[:D, :], 1, 0)

    for d in range(1, 5):
        for q in range(SUBS):
            if d < 4 or q < half:
                from_left(d - 1, q).wait_recv()
                if d < 3 or (d == 3 and q < half):
                    go(to_right(d, q))
                go(mate_copy(d, slot(y - d, c), q))
            b = SUBS - 1 - q
            if d < 4 or b >= half:
                from_right(d - 1, b).wait_recv()
                if d < 3 or (d == 3 and b >= half):
                    go(to_left(d, b))
                go(mate_copy(d if d == 4 else 8 - d, slot(y + d, c), b))
            if d < 4 and q == 0:
                own_part(d - 1)
                if d == 3:
                    own_part(3)
    for k in range(8):
        for q in range(SUBS):
            mate_copy(k, slot(y - k, o), q).wait_recv()

    def aggregated(g, _):
        cands = []
        for i in range(GROUP):
            t = g * GROUP + i
            v = jnp.concatenate([table[places[t * NBT + j]] for j in range(NBT)], axis=0)
            cand[at(t), :] = v
            cands.append(v)
        for i in range(GROUP):
            t = g * GROUP + i
            aggs[at(t), :] = (over(cn[at(t), :], cands[i], 1, 0) / DEG).astype(bf16)
        return 0

    def embedded(g, _):
        first = g * GROUP * TILE
        pre[...] = xw[at(g * GROUP, GROUP), :] + over(aggs[at(g * GROUP, GROUP), :], weight[D:, :], 1, 0)
        step = 64
        for r in range(0, GROUP * TILE, step):
            v = pre[r : r + step, :]
            gate = jax.nn.sigmoid(v)
            hid = v * gate
            scale = lax.rsqrt(jnp.mean(hid * hid, axis=-1, keepdims=True) + 1e-06)
            e = hid * scale
            where = pl.ds(pl.multiple_of(first + r, step), step)
            emb[where, :] = e
            eh[where, :] = e.astype(bf16)
            slope[where, :] = scale * (gate * (1.0 + v * (1.0 - gate)))
        return 0

    def scored(g, loss):
        scs = [over(cand[at(g * GROUP + i), :], eh[at(g * GROUP + i), :], 1, 1) * inv_root for i in range(GROUP)]
        for i in range(GROUP):
            t = g * GROUP + i
            sc = scs[i]
            nb = nbr[:, at(t)]
            ng = neg[:, at(t)]
            pos = nb[0:1, :] == kio
            ps = jnp.sum(jnp.where(pos, sc, 0.0), axis=0, keepdims=True)
            negs = [ng[n : n + 1, :] == kio for n in range(NNEG)]
            ns = [jnp.sum(jnp.where(m, sc, 0.0), axis=0, keepdims=True) for m in negs]
            ex = 0.5 + jnp.concatenate(ns, axis=0) - ps
            loss += jax.nn.softplus(ex) * 0.25
            w = jax.nn.sigmoid(ex) * 0.25
            wsum = jnp.sum(w, axis=0, keepdims=True)
            ds = jnp.where(negs[0], w[0:1, :], 0.0)
            for n in range(1, NNEG):
                ds += jnp.where(negs[n], w[n : n + 1, :], 0.0)
            ds = (ds - jnp.where(pos, wsum, 0.0)) * inv_root
            dss[at(t), :] = ds.astype(bf16)
        return loss

    def backed(g, _):
        ds = [over(dss[at(g * GROUP + i), :], cand[at(g * GROUP + i), :], 0, 0) for i in range(GROUP)]
        for i in range(GROUP):
            t = g * GROUP + i
            e = emb[at(t), :]
            m2 = jnp.mean(ds[i] * e, axis=-1, keepdims=True)
            dpres[at(t), :] = (slope[at(t), :] * (ds[i] - e * m2)).astype(bf16)
        return 0

    n = TILES // GROUP
    lax.fori_loop(0, n, aggregated, 0)
    lax.fori_loop(0, n, embedded, 0)
    loss = lax.fori_loop(0, n, scored, jnp.zeros((NNEG, TILE), f32))
    lossp[...] = jnp.broadcast_to(jnp.sum(loss, keepdims=True), (8, 128))
    lax.fori_loop(0, n, backed, 0)

    dp = dpres[...]
    for h in range(2):
        src = table[pl.ds(0, NBD)].reshape(NODES, D) if h == 0 else aggs[...]
        v = over(src, dp, 0, 0)
        for l in range(2):
            dw[l * 512 + h * 256 : l * 512 + h * 256 + 256, :] = v[:, l * 128 : l * 128 + 128]
    first = [
        remote(dw.at[rows(o * 512, 512), :], w0, ws.at[0, 0], wr.at[0, 0], mate),
        remote(lossp, lossb.at[0], ws.at[0, 1], wr.at[0, 1], mate),
    ]
    for copy in first:
        go(copy)

    def returned(g, _):
        di = over(dpres[at(g * GROUP, GROUP), :], weight[...], 1, 1)
        own[pl.ds(g * GROUP * NBT, GROUP * NBT)] = di[:, :D].reshape(GROUP * NBT, BLK, D)
        da = (di[:, D:] / DEG).astype(bf16)
        for i in range(GROUP):
            t = g * GROUP + i
            a = jnp.concatenate([dss[at(t), :], ct[at(t), :]], axis=1)
            b = jnp.concatenate([eh[at(t), :], da[i * TILE : (i + 1) * TILE, :]], axis=0)
            cg[pl.ds(t * NBT, NBT)] = over(a, b, 1, 0).reshape(NBT, BLK, D)
        return 0

    cg[NBD] = jnp.zeros((BLK, D), f32)

    def scatter(stage, src, base, r, buf, n, me, dev):
        buf[me] = src[rows(base + me * r, r), :]
        for k in range(1, n):
            to = lax.rem(me + k, n)
            go(remote(src.at[rows(base + to * r, r), :], buf.at[me], ws.at[stage, k], wr.at[stage, me], dev(k)))

    def arrived(stage, buf, n, me, dev):
        for k in range(1, n):
            who = lax.rem(me + k, n)
            remote(buf.at[who], buf.at[who], ws.at[stage, k], wr.at[stage, who], dev(k)).wait_recv()

    def spread(stage, src, buf, n, me, dev):
        buf[me] = src[...]
        for k in range(1, n):
            go(remote(src, buf.at[me], ws.at[stage, k], wr.at[stage, me], dev(k)))

    def summed(buf, n):
        v = buf[0]
        for i in range(1, n):
            v = v + buf[i]
        return v

    lz, lx, lossz, lossx = lossb.at[pl.ds(2, NZ)], lossb.at[pl.ds(10, NX)], lossb.at[14], lossb.at[15]

    def wa():
        for copy in first:
            copy.wait_recv()
        sum0[...] = dw[rows(c * 512, 512), :] + w0[...]
        lossb[1] = lossp[...] + lossb[0]
        scatter(1, sum0, 0, 32, a1, NZ, z, zs)
        scatter(2, sum0, 256, 64, b1, NX, x, xs)
        spread(3, lossb.at[1], lz, NZ, z, zs)

    def wb():
        arrived(2, b1, NX, x, xs)
        sum1[32:96, :] = summed(b1, NX)
        scatter(4, sum1, 32, 8, b2, NZ, z, zs)

    def wc():
        arrived(1, a1, NZ, z, zs)
        arrived(3, lz, NZ, z, zs)
        sum1[0:32, :] = summed(a1, NZ)
        lossb[14] = summed(lz, NZ)
        scatter(5, sum1, 0, 8, a2, NX, x, xs)
        spread(6, lossz, lx, NX, x, xs)

    def wd():
        arrived(4, b2, NZ, z, zs)
        arrived(5, a2, NX, x, xs)
        arrived(6, lx, NX, x, xs)
        sum2[0:8, :] = summed(a2, NX)
        sum2[8:16, :] = summed(b2, NZ)
        sum2[16:24, :] = summed(lx, NX)
        spread(7, sum2, ybuf, NY, y, ys)

    def we():
        arrived(7, ybuf, NY, y, ys)
        t = summed(ybuf, NY)
        total[...] = t
        loss_out[...] = t[16:24, :]
        spread(8, total.at[pl.ds(0, 8), :], ag2a, NX, x, xs)
        spread(9, total.at[pl.ds(8, 8), :], ag2b, NZ, z, zs)

    def wide(stage, src, r, base, n, me, dev):
        for k in range(1, n):
            go(remote(src, ag1.at[rows(base + me * r, r), :], ws.at[stage, k], wr.at[stage, me], dev(k)))

    def wide_arrived(stage, r, base, n, me, dev):
        for k in range(1, n):
            who = lax.rem(me + k, n)
            v = ag1.at[rows(base + who * r, r), :]
            remote(v, v, ws.at[stage, k], wr.at[stage, who], dev(k)).wait_recv()

    def wf():
        arrived(8, ag2a, NX, x, xs)
        for i in range(NX):
            sum3[i * 8 : i * 8 + 8, :] = ag2a[i]
        wide(10, sum3.at[pl.ds(0, 32), :], 32, 0, NZ, z, zs)
        ag1[rows(z * 32, 32), :] = sum3[0:32, :]

    def wg():
        arrived(9, ag2b, NZ, z, zs)
        for i in range(NZ):
            sum3[32 + i * 8 : 40 + i * 8, :] = ag2b[i]
        wide(11, sum3.at[pl.ds(32, 64), :], 64, 256, NX, x, xs)
        ag1[rows(256 + x * 64, 64), :] = sum3[32:96, :]

    last = []

    def wh():
        wide_arrived(11, 64, 256, NX, x, xs)
        last.append(go(remote(ag1.at[pl.ds(256, 256), :], dw_out.at[rows(c * 512 + 256, 256), :], ws.at[12, 1], wr.at[12, 1], mate)))
        dw_out[rows(c * 512 + 256, 256), :] = ag1[256:512, :]

    def wi():
        wide_arrived(10, 32, 0, NZ, z, zs)
        last.append(go(remote(ag1.at[pl.ds(0, 256), :], dw_out.at[rows(c * 512, 256), :], ws.at[12, 0], wr.at[12, 0], mate)))
        dw_out[rows(c * 512, 256), :] = ag1[0:256, :]


    order = [4, 3, -3, 2, -2, 1, -1, 0]

    def owner(k):
        return lax.rem(y + k + NY, NY)

    def grad_of(k, core, p):
        return cg[places[2 * NBD + (owner(k) * 2 + core) * NBND + p]]

    mcopies = {}

    def to_mate():
        for i, k in enumerate(order):
            for p in range(NBND):
                msend[i, p] = grad_of(k, o, p)
            mcopies[k] = go(remote(msend.at[i], mates.at[i], ms.at[i], mr.at[i], mate))

    ready = set()

    def summed_block(k, p):
        return grad_of(k, c, p) + mates[order.index(k), p]

    def wait_mate(k):
        if k not in ready:
            mcopies[k].wait_recv()
            ready.add(k)

    def hop(to_right, s, h):
        sb, rb, ss, rsm, dev = (rsend, rbuf, rs, rr, right) if to_right else (lsend, lbuf, ls, lr, left)
        view = pl.ds(h * HALF, HALF)
        return remote(sb.at[s, view], rb.at[s, view], ss.at[s, h], rsm.at[s, h], dev)

    def ring(to_right, s, h):
        start = 0 if (h == 0) == to_right else 1
        k = 4 - s if to_right else (-(4 - s) if s else 4)
        wait_mate(k)
        if s > start:
            hop(to_right, s - 1, h).wait_recv()
        for p in range(h * HALF, (h + 1) * HALF):
            v = summed_block(k, p)
            if s > start:
                v = v + (rbuf if to_right else lbuf)[s - 1, p]
            (rsend if to_right else lsend)[s, p] = v
        go(hop(to_right, s, h))

    def ringed(s, h):
        def run():
            ring(True, s, h)
            ring(False, s, 1 - h)

        return run

    def r4():
        wait_mate(0)
        for h in (1, 0):
            hop(True, 3, h).wait_recv()
            hop(False, 3, 1 - h).wait_recv()
        for p in range(NBND):
            out[p] = summed_block(0, p) + rbuf[3, p] + lbuf[3, p]

    results = []

    def own_sum():
        def body(g, _):
            for i in range(8):
                b = g * 8 + i
                own[b] = own[b] + cg[places[NBD + b]]
            return 0

        lax.fori_loop(0, NBD // 8, body, 0)
        copy = pltpu.make_async_copy(own, own_out, osem)
        copy.start()
        results.append(copy)

    lax.fori_loop(0, n // 2, returned, 0)
    wa()
    lax.fori_loop(n // 2, n, returned, 0)
    to_mate()
    for step in (
        ringed(0, 0), ringed(1, 1), wb, own_sum, wc, ringed(1, 0), wd, ringed(2, 1), we, ringed(2, 0),
        ringed(3, 1), wg, wf, ringed(3, 0), wh, wi, r4,
    ):
        step()
    for copy in last:
        copy.wait_recv()
    for copy in sent:
        copy.wait_send()
    for copy in results:
        copy.wait()


def layer(places, boundary, nbr, neg, weight, features):
    vm = pl.BlockSpec(memory_space=pltpu.VMEM)
    sm = pl.BlockSpec(memory_space=pltpu.SMEM)
    hbm = pl.BlockSpec(memory_space=pl.ANY)
    V = pltpu.VMEM
    sem = pltpu.SemaphoreType.DMA
    return pl.pallas_call(
        layer_kernel,
        out_shape=(
            jax.ShapeDtypeStruct((NBD, BLK, D), f32),
            jax.ShapeDtypeStruct((NBND, BLK, D), f32),
            jax.ShapeDtypeStruct((1024, 128), f32),
            jax.ShapeDtypeStruct((8, 128), f32),
        ),
        in_specs=[sm, sm, vm, vm, vm, hbm],
        out_specs=(hbm, vm, vm, vm),
        scratch_shapes=[
            V((TABLE // BLK, BLK, D), bf16),
            V((NODES, D), bf16),
            V((NODES, TILE), bf16),
            V((NODES, TILE), bf16),
            V((NODES, D), f32),
            V((NODES, D), bf16),
            V((NODES, D), f32),
            V((NODES, D), f32),
            V((NODES, D), bf16),
            V((NODES, TILE), bf16),
            V((NODES, D), bf16),
            V((NBD, BLK, D), f32),
            V((NBD + 1, BLK, D), f32),
            V((GROUP * TILE, D), f32),
            V((8, NBND, BLK, D), f32),
            V((8, NBND, BLK, D), f32),
            V((4, NBND, BLK, D), f32),
            V((4, NBND, BLK, D), f32),
            V((4, NBND, BLK, D), f32),
            V((4, NBND, BLK, D), f32),
            V((1024, 128), f32),
            V((8, 128), f32),
            V((512, 128), f32),
            V((512, 128), f32),
            V((16, 8, 128), f32),
            V((NZ, 32, 128), f32),
            V((NX, 64, 128), f32),
            V((NX, 8, 128), f32),
            V((NZ, 8, 128), f32),
            V((96, 128), f32),
            V((96, 128), f32),
            V((24, 128), f32),
            V((NY, 24, 128), f32),
            V((24, 128), f32),
            V((NX, 8, 128), f32),
            V((NZ, 8, 128), f32),
            V((512, 128), f32),
            sem(()),
            sem(()),
            sem((4, SUBS)),
            sem((4, SUBS)),
            sem((4, SUBS)),
            sem((4, SUBS)),
            sem((8, SUBS)),
            sem((8, SUBS)),
            sem((8,)),
            sem((8,)),
            sem((4, 2)),
            sem((4, 2)),
            sem((4, 2)),
            sem((4, 2)),
            sem((13, 8)),
            sem((13, 8)),
        ],
        compiler_params=pltpu.CompilerParams(collective_id=0, has_side_effects=True),
        name="layer",
    )(places, boundary, nbr, neg, weight, features)


def add_kernel(boundary, lossin, got, dwt, own, out, wgrad, loss, buf, sems):
    parts = 4
    n = NBD // parts
    for i in range(parts):
        pltpu.make_async_copy(own.at[pl.ds(i * n, n)], buf.at[pl.ds(i * n, n)], sems.at[i]).start()
    wgrad[:, 0:128] = dwt[0:512, :] / NODES
    wgrad[:, 128:256] = dwt[512:1024, :] / NODES
    loss[0] = lossin[0, 0] / (NODES * 512)
    for i in range(parts):
        pltpu.make_async_copy(own.at[pl.ds(i * n, n)], buf.at[pl.ds(i * n, n)], sems.at[i]).wait()
    for p in range(NBND):
        b = boundary[p]
        buf[b] = buf[b] + got[p]
    for i in range(parts):
        pltpu.make_async_copy(buf.at[pl.ds(i * n, n)], out.at[pl.ds(i * n, n)], sems.at[i]).start()
    for i in range(parts):
        pltpu.make_async_copy(buf.at[pl.ds(i * n, n)], out.at[pl.ds(i * n, n)], sems.at[i]).wait()


def added(boundary, lossin, got, dwt, own):
    hbm = pl.BlockSpec(memory_space=pl.ANY)
    vm = pl.BlockSpec(memory_space=pltpu.VMEM)
    sm = pl.BlockSpec(memory_space=pltpu.SMEM)
    return pl.pallas_call(
        add_kernel,
        out_shape=(
            jax.ShapeDtypeStruct((NBD, BLK, D), f32),
            jax.ShapeDtypeStruct((512, 256), f32),
            jax.ShapeDtypeStruct((1,), f32),
        ),
        in_specs=[sm, sm, vm, vm, hbm],
        out_specs=(hbm, vm, sm),
        scratch_shapes=[pltpu.VMEM((NBD, BLK, D), f32), pltpu.SemaphoreType.DMA((4,))],
        name="add_returned",
    )(boundary, lossin, got, dwt, own)


def per_device(features, boundary, request, tile_slots, neighbors, negatives, layer_weight):
    places = indices(tile_slots.T, request.T)
    own, got, dwt, losst = layer(
        places, boundary, neighbors.T, negatives.T, layer_weight, features.reshape(NBD, BLK, D)
    )
    grad, wgrad, loss = added(boundary, losst, got, dwt, own)
    return grad.reshape(NODES, D), wgrad, loss.reshape(())


def solution(mesh):
    finer = Mesh(mesh.devices.reshape(NZ, NX, NY, 2), AXES)
    dg = AXES
    return jax.shard_map(
        per_device,
        mesh=finer,
        in_specs=(P(dg, None), P(dg), P(dg, None), P(dg, None), P(dg, None), P(dg, None), P()),
        out_specs=(P(dg, None), P(), P()),
        check_vma=False,
    )
```

```python
import functools

import jax
import jax.numpy as jnp
from jax import lax
from jax.experimental import pallas as pl
from jax.experimental.pallas import tpu as pltpu
from jax.sharding import Mesh
from jax.sharding import PartitionSpec as P

MESH = pl.DeviceIdType.MESH
TILE = 128
BLK = 16
NBT = 8
DEG = 10
NNEG = 4
CAP = 6
TILES = 16
NODES = 2048
D = 256
NBD = 128
NBND = 16
ROWS = NBND * BLK
PEERS = 16
TABLE = NODES + PEERS * ROWS
NY = 8
NZ = 8
NX = 4
f32 = jnp.float32
bf16 = jnp.bfloat16
AXES = ("z", "x", "y", "c")


def place():
    return tuple(lax.axis_index(a) for a in AXES)


def remote(src, dst, send, recv, device):
    return pltpu.make_async_remote_copy(
        src_ref=src, dst_ref=dst, send_sem=send, recv_sem=recv, device_id=device, device_id_type=MESH
    )


SUBS = 4
SUB = NBND // SUBS
HALF = NBND // 2
GROUP = 4


def over(a, b, da, db):
    return lax.dot_general(a, b, (((da,), (db,)), ((), ())), preferred_element_type=f32)


def layer_kernel(
    slots, req, boundary, nbr, neg, weight, feat,
    own, out, dw_out, loss_out,
    table, pack, places, invv, inv, cand, ct, cn, xw, aggs, emb, slope, eh, dss, wn, dpres, cg, pre,
    msend, mates, rbuf, lbuf, rsend, lsend,
    dw, lossp, w0, sum0, lossb, a1, b1, a2, b2, sum1, sum3, sum2, ybuf, total, ag2a, ag2b, ag1,
    fsem, psem, isem, grs, grr, gls, glr, gcs, gcr, ms, mr, rs, rr, ls, lr, ws, wr,
):
    z, x, y, c = place()
    o = 1 - c
    right = (z, x, lax.rem(y + 1, NY), c)
    left = (z, x, lax.rem(y + NY - 1, NY), c)
    mate = (z, x, y, o)

    def zs(k):
        return (lax.rem(z + k, NZ), x, y, c)

    def xs(k):
        return (z, lax.rem(x + k, NX), y, c)

    def ys(k):
        return (z, x, lax.rem(y + k, NY), c)

    sent = []

    def go(copy):
        copy.start()
        sent.append(copy)
        return copy

    def rows(first, n):
        return pl.ds(pl.multiple_of(first, 8), n)

    def slot(yy, cc):
        return NBD + (lax.rem(yy + NY, NY) * 2 + cc) * NBND

    peers = [mate] + [zs(k) for k in range(1, NZ)] + [xs(k) for k in range(1, NX)] + [ys(k) for k in range(1, NY)]
    barrier = pltpu.get_barrier_semaphore()
    for d in peers:
        pl.semaphore_signal(barrier, inc=1, device_id=d, device_id_type=MESH)
    loads = [
        pltpu.make_async_copy(feat, pack, psem),
        pltpu.make_async_copy(feat, table.at[pl.ds(0, NBD)], fsem),
    ]
    for copy in loads:
        copy.start()
    me = slot(y, c)

    kio = lax.broadcasted_iota(jnp.int32, (TILE, TILE), 0)
    inv_root = D ** (-0.5)

    def at(t, n=1):
        return pl.ds(t * TILE if isinstance(t, int) else pl.multiple_of(t * TILE, TILE), n * TILE)

    def counted(g, _):
        for i in range(2):
            t = g * 2 + i
            nb = nbr[:, at(t)]
            v = jnp.zeros((TILE, TILE), f32)
            for j in range(DEG):
                v += jnp.where(nb[j : j + 1, :] == kio, 1.0, 0.0)
            ct[at(t), :] = v.astype(bf16)
            cn[at(t), :] = v.T.astype(bf16)
        return 0

    lax.fori_loop(0, TILES // 2, counted, 0)
    loads[0].wait()
    for p in range(NBND):
        table[me + p] = pack[boundary[p]]
    pl.semaphore_wait(barrier, len(peers))

    def piece(s, q):
        return table.at[pl.ds(s + q * SUB, SUB)]

    def to_right(d, q):
        v = piece(slot(y - d, c), q)
        return remote(v, v, grs.at[d, q], grr.at[d, q], right)

    def from_left(d, q):
        v = piece(slot(y - 1 - d, c), q)
        return remote(v, v, grs.at[d, q], grr.at[d, q], right)

    def to_left(d, q):
        v = piece(slot(y + d, c), q)
        return remote(v, v, gls.at[d, q], glr.at[d, q], left)

    def from_right(d, q):
        v = piece(slot(y + 1 + d, c), q)
        return remote(v, v, gls.at[d, q], glr.at[d, q], left)

    def mate_copy(k, s, q):
        v = piece(s, q)
        return remote(v, v, gcs.at[k, q], gcr.at[k, q], mate)

    half = SUBS // 2
    for q in range(SUBS):
        go(to_right(0, q))
        go(to_left(0, SUBS - 1 - q))
    for q in range(SUBS):
        go(mate_copy(0, me, q))

    spot = lax.broadcasted_iota(jnp.int32, (8, 128), 0) * 128 + lax.broadcasted_iota(jnp.int32, (8, 128), 1)

    def placed(t, back):
        for j in range(NBT):
            s = slots[j, t]
            n = jnp.maximum(s - NBD, 0)
            e = (n * 43) >> 8
            b = jnp.where(s < NBD, s, NBD + e * NBND + req[n - e * CAP, e])
            places[t * NBT + j] = b
            back = jnp.where(spot == b, t * NBT + j, back)
        return back

    invv[...] = lax.fori_loop(0, TILES, placed, jnp.full((8, 128), NBD, jnp.int32))
    down = pltpu.make_async_copy(invv, inv, isem)
    down.start()
    loads[1].wait()

    def own_part(g):
        v = table[pl.ds(g * GROUP * NBT, GROUP * NBT)].reshape(GROUP * TILE, D)
        xw[at(g * GROUP, GROUP), :] = over(v, weight[:D, :], 1, 0)

    for d in range(1, 5):
        for q in range(SUBS):
            if d < 4 or q < half:
                from_left(d - 1, q).wait_recv()
                if d < 3 or (d == 3 and q < half):
                    go(to_right(d, q))
                go(mate_copy(d, slot(y - d, c), q))
            b = SUBS - 1 - q
            if d < 4 or b >= half:
                from_right(d - 1, b).wait_recv()
                if d < 3 or (d == 3 and b >= half):
                    go(to_left(d, b))
                go(mate_copy(d if d == 4 else 8 - d, slot(y + d, c), b))
            if d < 4 and q == 0:
                own_part(d - 1)
                if d == 3:
                    own_part(3)
    for k in range(8):
        for q in range(SUBS):
            mate_copy(k, slot(y - k, o), q).wait_recv()

    down.wait()

    def aggregated(g, _):
        cands = []
        for i in range(GROUP):
            t = g * GROUP + i
            v = jnp.concatenate([table[places[t * NBT + j]] for j in range(NBT)], axis=0)
            cand[at(t), :] = v
            cands.append(v)
        for i in range(GROUP):
            t = g * GROUP + i
            aggs[at(t), :] = (over(cn[at(t), :], cands[i], 1, 0) / DEG).astype(bf16)
        return 0

    def embedded(g, _):
        first = g * GROUP * TILE
        pre[g % 2] = xw[at(g * GROUP, GROUP), :] + over(aggs[at(g * GROUP, GROUP), :], weight[D:, :], 1, 0)
        step = 32
        for r in range(0, GROUP * TILE, step):
            v = pre[g % 2, r : r + step, :]
            gate = jax.nn.sigmoid(v)
            hid = v * gate
            scale = lax.rsqrt(jnp.mean(hid * hid, axis=-1, keepdims=True) + 1e-06)
            e = hid * scale
            where = pl.ds(first + r, step)
            emb[where, :] = e
            eh[where, :] = e.astype(bf16)
            slope[where, :] = scale * (gate * (1.0 + v * (1.0 - gate)))
        return 0

    def scored(g, loss):
        scs = [over(cand[at(g * GROUP + i), :], eh[at(g * GROUP + i), :], 1, 1) * inv_root for i in range(GROUP)]
        for i in range(GROUP):
            t = g * GROUP + i
            sc = scs[i]
            nb = nbr[:, at(t)]
            ng = neg[:, at(t)]
            ps = jnp.sum(jnp.where(nb[0:1, :] == kio, sc, 0.0), axis=0, keepdims=True)
            ns = [jnp.sum(jnp.where(ng[n : n + 1, :] == kio, sc, 0.0), axis=0, keepdims=True) for n in range(NNEG)]
            ex = 0.5 + jnp.concatenate(ns, axis=0) - ps
            loss += jax.nn.softplus(ex) * 0.25
            w = jax.nn.sigmoid(ex) * 0.25
            wn[t] = jnp.concatenate([w, jnp.sum(w, axis=0, keepdims=True), jnp.zeros((3, TILE), f32)], axis=0)
        return loss

    def backed(g, _):
        for i in range(GROUP):
            t = g * GROUP + i
            ng = neg[:, at(t)]
            v = jnp.where(nbr[0:1, at(t)] == kio, -wn[t, 4:5, :], 0.0)
            for n in range(NNEG):
                v += jnp.where(ng[n : n + 1, :] == kio, wn[t, n : n + 1, :], 0.0)
            dss[at(t), :] = (v * inv_root).astype(bf16)
        ds = [over(dss[at(g * GROUP + i), :], cand[at(g * GROUP + i), :], 0, 0) for i in range(GROUP)]
        for i in range(GROUP):
            t = g * GROUP + i
            e = emb[at(t), :]
            m2 = jnp.mean(ds[i] * e, axis=-1, keepdims=True)
            dpres[at(t), :] = (slope[at(t), :] * (ds[i] - e * m2)).astype(bf16)
        return 0

    n = TILES // GROUP
    loss = jnp.zeros((NNEG, TILE), f32)
    for step in range(n + 3):
        if step >= 3:
            backed(step - 3, 0)
        if 2 <= step < n + 2:
            loss = scored(step - 2, loss)
        if 1 <= step < n + 1:
            embedded(step - 1, 0)
        if step < n:
            aggregated(step, 0)
    lossp[...] = jnp.broadcast_to(jnp.sum(loss, keepdims=True), (8, 128))

    dp = dpres[...]
    for h in range(2):
        src = table[pl.ds(0, NBD)].reshape(NODES, D) if h == 0 else aggs[...]
        v = over(src, dp, 0, 0)
        for l in range(2):
            dw[l * 512 + h * 256 : l * 512 + h * 256 + 256, :] = v[:, l * 128 : l * 128 + 128]
    first = [
        remote(dw.at[rows(o * 512, 512), :], w0, ws.at[0, 0], wr.at[0, 0], mate),
        remote(lossp, lossb.at[0], ws.at[0, 1], wr.at[0, 1], mate),
    ]
    for copy in first:
        go(copy)

    def returned(g, _):
        di = over(dpres[at(g * GROUP, GROUP), :], weight[...], 1, 1)
        own[pl.ds(g * GROUP * NBT, GROUP * NBT)] = di[:, :D].reshape(GROUP * NBT, BLK, D)
        da = (di[:, D:] / DEG).astype(bf16)
        for i in range(GROUP):
            t = g * GROUP + i
            a = jnp.concatenate([dss[at(t), :], ct[at(t), :]], axis=1)
            b = jnp.concatenate([eh[at(t), :], da[i * TILE : (i + 1) * TILE, :]], axis=0)
            cg[pl.ds(t * NBT, NBT)] = over(a, b, 1, 0).reshape(NBT, BLK, D)
        return 0

    cg[NBD] = jnp.zeros((BLK, D), f32)

    def others(n):
        return sorted(range(1, n), key=lambda k: -min(k, n - k))

    def scatter(stage, src, base, r, buf, n, me, dev):
        buf[me] = src[rows(base + me * r, r), :]
        for k in others(n):
            to = lax.rem(me + k, n)
            go(remote(src.at[rows(base + to * r, r), :], buf.at[me], ws.at[stage, k], wr.at[stage, me], dev(k)))

    def arrived(stage, buf, n, me, dev):
        for k in range(1, n):
            who = lax.rem(me + k, n)
            remote(buf.at[who], buf.at[who], ws.at[stage, k], wr.at[stage, who], dev(k)).wait_recv()

    def spread(stage, src, buf, n, me, dev):
        buf[me] = src[...]
        for k in others(n):
            go(remote(src, buf.at[me], ws.at[stage, k], wr.at[stage, me], dev(k)))

    def summed(buf, n):
        v = buf[0]
        for i in range(1, n):
            v = v + buf[i]
        return v

    lz, lx, lossz, lossx = lossb.at[pl.ds(2, NZ)], lossb.at[pl.ds(10, NX)], lossb.at[14], lossb.at[15]

    def wa():
        for copy in first:
            copy.wait_recv()
        sum0[...] = dw[rows(c * 512, 512), :] + w0[...]
        lossb[1] = lossp[...] + lossb[0]
        scatter(1, sum0, 0, 32, a1, NZ, z, zs)
        scatter(2, sum0, 256, 64, b1, NX, x, xs)
        spread(3, lossb.at[1], lz, NZ, z, zs)

    def wb():
        arrived(2, b1, NX, x, xs)
        sum1[32:96, :] = summed(b1, NX)
        scatter(4, sum1, 32, 8, b2, NZ, z, zs)

    def wc():
        arrived(1, a1, NZ, z, zs)
        arrived(3, lz, NZ, z, zs)
        sum1[0:32, :] = summed(a1, NZ)
        lossb[14] = summed(lz, NZ)
        scatter(5, sum1, 0, 8, a2, NX, x, xs)
        spread(6, lossz, lx, NX, x, xs)

    def wd():
        arrived(4, b2, NZ, z, zs)
        arrived(5, a2, NX, x, xs)
        arrived(6, lx, NX, x, xs)
        sum2[0:8, :] = summed(a2, NX)
        sum2[8:16, :] = summed(b2, NZ)
        sum2[16:24, :] = summed(lx, NX)
        spread(7, sum2, ybuf, NY, y, ys)

    def we():
        arrived(7, ybuf, NY, y, ys)
        t = summed(ybuf, NY)
        total[...] = t
        loss_out[...] = t[16:24, :]
        spread(8, total.at[pl.ds(0, 8), :], ag2a, NX, x, xs)
        spread(9, total.at[pl.ds(8, 8), :], ag2b, NZ, z, zs)

    def wide(stage, src, r, base, n, me, dev):
        for k in others(n):
            go(remote(src, ag1.at[rows(base + me * r, r), :], ws.at[stage, k], wr.at[stage, me], dev(k)))

    def wide_arrived(stage, r, base, n, me, dev):
        for k in range(1, n):
            who = lax.rem(me + k, n)
            v = ag1.at[rows(base + who * r, r), :]
            remote(v, v, ws.at[stage, k], wr.at[stage, who], dev(k)).wait_recv()

    def wf():
        arrived(8, ag2a, NX, x, xs)
        for i in range(NX):
            sum3[i * 8 : i * 8 + 8, :] = ag2a[i]
        wide(10, sum3.at[pl.ds(0, 32), :], 32, 0, NZ, z, zs)
        ag1[rows(z * 32, 32), :] = sum3[0:32, :]

    def wg():
        arrived(9, ag2b, NZ, z, zs)
        for i in range(NZ):
            sum3[32 + i * 8 : 40 + i * 8, :] = ag2b[i]
        wide(11, sum3.at[pl.ds(32, 64), :], 64, 256, NX, x, xs)
        ag1[rows(256 + x * 64, 64), :] = sum3[32:96, :]

    last = []

    def wh():
        wide_arrived(11, 64, 256, NX, x, xs)
        last.append(go(remote(ag1.at[pl.ds(256, 256), :], dw_out.at[rows(c * 512 + 256, 256), :], ws.at[12, 1], wr.at[12, 1], mate)))
        dw_out[rows(c * 512 + 256, 256), :] = ag1[256:512, :]

    def wi():
        wide_arrived(10, 32, 0, NZ, z, zs)
        last.append(go(remote(ag1.at[pl.ds(0, 256), :], dw_out.at[rows(c * 512, 256), :], ws.at[12, 0], wr.at[12, 0], mate)))
        dw_out[rows(c * 512, 256), :] = ag1[0:256, :]


    order = [4, 3, -3, 2, -2, 1, -1, 0]

    def owner(k):
        return lax.rem(y + k + NY, NY)

    def grad_of(k, core, p):
        q = (owner(k) * 2 + core) * NBND + p
        return cg[inv[1 + q // 128, q % 128]]

    mcopies = {}

    def to_mate():
        for i, k in enumerate(order):
            for p in range(NBND):
                msend[i, p] = grad_of(k, o, p)
            mcopies[k] = go(remote(msend.at[i], mates.at[i], ms.at[i], mr.at[i], mate))

    ready = set()

    def summed_block(k, p):
        return grad_of(k, c, p) + mates[order.index(k), p]

    def wait_mate(k):
        if k not in ready:
            mcopies[k].wait_recv()
            ready.add(k)

    def hop(to_right, s, h):
        sb, rb, ss, rsm, dev = (rsend, rbuf, rs, rr, right) if to_right else (lsend, lbuf, ls, lr, left)
        view = pl.ds(h * HALF, HALF)
        return remote(sb.at[s, view], rb.at[s, view], ss.at[s, h], rsm.at[s, h], dev)

    def ring(to_right, s, h):
        start = 0 if (h == 0) == to_right else 1
        k = 4 - s if to_right else (-(4 - s) if s else 4)
        wait_mate(k)
        if s > start:
            hop(to_right, s - 1, h).wait_recv()
        for p in range(h * HALF, (h + 1) * HALF):
            v = summed_block(k, p)
            if s > start:
                v = v + (rbuf if to_right else lbuf)[s - 1, p]
            (rsend if to_right else lsend)[s, p] = v
        go(hop(to_right, s, h))

    def ringed(s, h):
        def run():
            ring(True, s, h)
            ring(False, s, 1 - h)

        return run

    def r4():
        wait_mate(0)
        for h in (1, 0):
            hop(True, 3, h).wait_recv()
            hop(False, 3, 1 - h).wait_recv()
        for p in range(NBND):
            out[p] = summed_block(0, p) + rbuf[3, p] + lbuf[3, p]

    def own_sum():
        def body(g, _):
            for i in range(8):
                b = g * 8 + i
                own[b] = own[b] + cg[inv[0, b]]
            return 0

        lax.fori_loop(0, NBD // 8, body, 0)

    lax.fori_loop(0, n // 2, returned, 0)
    wa()
    lax.fori_loop(n // 2, n, returned, 0)
    to_mate()
    for step in (
        ringed(0, 0), ringed(1, 1), wb, own_sum, wc, ringed(1, 0), wd, ringed(2, 1), we, ringed(2, 0),
        ringed(3, 1), wg, wf, ringed(3, 0), wh, wi, r4,
    ):
        step()
    for copy in last:
        copy.wait_recv()
    for copy in sent:
        copy.wait_send()


def layer(slots, req, boundary, nbr, neg, weight, features):
    vm = pl.BlockSpec(memory_space=pltpu.VMEM)
    sm = pl.BlockSpec(memory_space=pltpu.SMEM)
    hbm = pl.BlockSpec(memory_space=pl.ANY)
    V = pltpu.VMEM
    sem = pltpu.SemaphoreType.DMA
    return pl.pallas_call(
        layer_kernel,
        out_shape=(
            pltpu.VMEM((NBD, BLK, D), f32),
            pltpu.VMEM((NBND, BLK, D), f32),
            pltpu.VMEM((1024, 128), f32),
            jax.ShapeDtypeStruct((8, 128), f32),
        ),
        in_specs=[sm, sm, sm, vm, vm, vm, hbm],
        out_specs=(vm, vm, vm, vm),
        scratch_shapes=[
            V((TABLE // BLK, BLK, D), bf16),
            V((NBD, BLK, D), bf16),
            pltpu.SMEM((NBD,), jnp.int32),
            V((8, 128), jnp.int32),
            pltpu.SMEM((8, 128), jnp.int32),
            V((NODES, D), bf16),
            V((NODES, TILE), bf16),
            V((NODES, TILE), bf16),
            V((NODES, D), f32),
            V((NODES, D), bf16),
            V((NODES, D), f32),
            V((NODES, D), f32),
            V((NODES, D), bf16),
            V((NODES, TILE), bf16),
            V((TILES, 8, TILE), f32),
            V((NODES, D), bf16),
            V((NBD + 1, BLK, D), f32),
            V((2, GROUP * TILE, D), f32),
            V((8, NBND, BLK, D), f32),
            V((8, NBND, BLK, D), f32),
            V((4, NBND, BLK, D), f32),
            V((4, NBND, BLK, D), f32),
            V((4, NBND, BLK, D), f32),
            V((4, NBND, BLK, D), f32),
            V((1024, 128), f32),
            V((8, 128), f32),
            V((512, 128), f32),
            V((512, 128), f32),
            V((16, 8, 128), f32),
            V((NZ, 32, 128), f32),
            V((NX, 64, 128), f32),
            V((NX, 8, 128), f32),
            V((NZ, 8, 128), f32),
            V((96, 128), f32),
            V((96, 128), f32),
            V((24, 128), f32),
            V((NY, 24, 128), f32),
            V((24, 128), f32),
            V((NX, 8, 128), f32),
            V((NZ, 8, 128), f32),
            V((512, 128), f32),
            sem(()),
            sem(()),
            sem(()),
            sem((4, SUBS)),
            sem((4, SUBS)),
            sem((4, SUBS)),
            sem((4, SUBS)),
            sem((8, SUBS)),
            sem((8, SUBS)),
            sem((8,)),
            sem((8,)),
            sem((4, 2)),
            sem((4, 2)),
            sem((4, 2)),
            sem((4, 2)),
            sem((13, 8)),
            sem((13, 8)),
        ],
        compiler_params=pltpu.CompilerParams(collective_id=0, has_side_effects=True),
        name="layer",
    )(slots, req, boundary, nbr, neg, weight, features)


def add_kernel(boundary, lossin, got, dwt, own, out, wgrad, loss, buf, wg, sems):
    parts = 4
    n = NBD // parts
    @pl.loop(0, 16)
    def _(i):
        buf[pl.ds(i * 8, 8)] = own[pl.ds(i * 8, 8)]

    for p in range(NBND):
        b = boundary[p]
        buf[b] = buf[b] + got[p]
    outs = [pltpu.make_async_copy(buf.at[pl.ds(i * n, n)], out.at[pl.ds(i * n, n)], sems.at[i]) for i in range(parts)]
    for copy in outs:
        copy.start()
    loss[0] = lossin[0, 0] / (NODES * 512)
    wg[:, 0:128] = dwt[0:512, :] / NODES
    wg[:, 128:256] = dwt[512:1024, :] / NODES
    outs.append(pltpu.make_async_copy(wg, wgrad, sems.at[parts]))
    outs[-1].start()
    for copy in outs:
        copy.wait()


def added(boundary, lossin, got, dwt, own):
    hbm = pl.BlockSpec(memory_space=pl.ANY)
    sm = pl.BlockSpec(memory_space=pltpu.SMEM)
    vm = pl.BlockSpec(memory_space=pltpu.VMEM)
    here = [pltpu.with_memory_space_constraint(v, pltpu.VMEM) for v in (got, dwt, own)]
    return pl.pallas_call(
        add_kernel,
        out_shape=(
            jax.ShapeDtypeStruct((NBD, BLK, D), f32),
            jax.ShapeDtypeStruct((512, 256), f32),
            jax.ShapeDtypeStruct((1,), f32),
        ),
        in_specs=[sm, sm, vm, vm, vm],
        out_specs=(hbm, hbm, sm),
        scratch_shapes=[
            pltpu.VMEM((NBD, BLK, D), f32),
            pltpu.VMEM((512, 256), f32),
            pltpu.SemaphoreType.DMA((6,)),
        ],
        name="add_returned",
    )(boundary, lossin, *here)


def per_device(features, boundary, request, tile_slots, neighbors, negatives, layer_weight):
    own, got, dwt, losst = layer(
        tile_slots.T, request.T, boundary, neighbors.T, negatives.T, layer_weight, features.reshape(NBD, BLK, D)
    )
    grad, wgrad, loss = added(boundary, losst, got, dwt, own)
    return grad.reshape(NODES, D), wgrad, loss.reshape(())


def solution(mesh):
    finer = Mesh(mesh.devices.reshape(NZ, NX, NY, 2), AXES)
    dg = AXES
    return jax.shard_map(
        per_device,
        mesh=finer,
        in_specs=(P(dg, None), P(dg), P(dg, None), P(dg, None), P(dg, None), P(dg, None), P()),
        out_specs=(P(dg, None), P(), P()),
        check_vma=False,
    )
```

```python
import functools

import jax
import jax.numpy as jnp
from jax import lax
from jax.experimental import pallas as pl
from jax.experimental.pallas import tpu as pltpu
from jax.sharding import Mesh
from jax.sharding import PartitionSpec as P

MESH = pl.DeviceIdType.MESH
TILE = 128
BLK = 16
NBT = 8
DEG = 10
NNEG = 4
CAP = 6
TILES = 16
NODES = 2048
D = 256
NBD = 128
NBND = 16
ROWS = NBND * BLK
PEERS = 16
TABLE = NODES + PEERS * ROWS
NY = 8
NZ = 8
NX = 4
f32 = jnp.float32
bf16 = jnp.bfloat16
AXES = ("z", "x", "y", "c")


def place():
    return tuple(lax.axis_index(a) for a in AXES)


def remote(src, dst, send, recv, device):
    return pltpu.make_async_remote_copy(
        src_ref=src, dst_ref=dst, send_sem=send, recv_sem=recv, device_id=device, device_id_type=MESH
    )


SUBS = 4
SUB = NBND // SUBS
HALF = NBND // 2
GROUP = 4


def over(a, b, da, db):
    return lax.dot_general(a, b, (((da,), (db,)), ((), ())), preferred_element_type=f32)


def layer_kernel(
    slots, req, boundary, nbr, neg, weight, feat,
    own, out, dw_out, loss_out,
    table, pack, places, invv, inv, cand, ct, cn, xw, aggs, emb, slope, eh, dss, wn, dpres, cg, pre,
    msend, mates, rbuf, lbuf, rsend, lsend,
    dw, lossp, w0, sum0, lossb, a1, b1, a2, b2, sum1, sum3, sum2, ybuf, total, ag2a, ag2b, ag1,
    fsem, psem, isem, grs, grr, gls, glr, gcs, gcr, ms, mr, rs, rr, ls, lr, ws, wr,
):
    z, x, y, c = place()
    o = 1 - c
    right = (z, x, lax.rem(y + 1, NY), c)
    left = (z, x, lax.rem(y + NY - 1, NY), c)
    mate = (z, x, y, o)

    def zs(k):
        return (lax.rem(z + k, NZ), x, y, c)

    def xs(k):
        return (z, lax.rem(x + k, NX), y, c)

    def ys(k):
        return (z, x, lax.rem(y + k, NY), c)

    sent = []

    def go(copy):
        copy.start()
        sent.append(copy)
        return copy

    def rows(first, n):
        return pl.ds(pl.multiple_of(first, 8), n)

    def slot(yy, cc):
        return NBD + (lax.rem(yy + NY, NY) * 2 + cc) * NBND

    peers = [mate] + [zs(k) for k in range(1, NZ)] + [xs(k) for k in range(1, NX)] + [ys(k) for k in range(1, NY)]
    barrier = pltpu.get_barrier_semaphore()
    for d in peers:
        pl.semaphore_signal(barrier, inc=1, device_id=d, device_id_type=MESH)
    loads = [
        pltpu.make_async_copy(feat, pack, psem),
        pltpu.make_async_copy(feat, table.at[pl.ds(0, NBD)], fsem),
    ]
    for copy in loads:
        copy.start()
    me = slot(y, c)

    kio = lax.broadcasted_iota(jnp.int32, (TILE, TILE), 0)
    inv_root = D ** (-0.5)

    def at(t, n=1):
        return pl.ds(t * TILE if isinstance(t, int) else pl.multiple_of(t * TILE, TILE), n * TILE)

    def counted(g, _):
        for i in range(2):
            t = g * 2 + i
            nb = nbr[:, at(t)]
            v = jnp.zeros((TILE, TILE), f32)
            for j in range(DEG):
                v += jnp.where(nb[j : j + 1, :] == kio, 1.0, 0.0)
            ct[at(t), :] = v.astype(bf16)
            cn[at(t), :] = v.T.astype(bf16)
        return 0

    loads[0].wait()
    for p in range(NBND):
        table[me + p] = pack[boundary[p]]
    pl.semaphore_wait(barrier, len(peers))

    def piece(s, q):
        return table.at[pl.ds(s + q * SUB, SUB)]

    def to_right(d, q):
        v = piece(slot(y - d, c), q)
        return remote(v, v, grs.at[d, q], grr.at[d, q], right)

    def from_left(d, q):
        v = piece(slot(y - 1 - d, c), q)
        return remote(v, v, grs.at[d, q], grr.at[d, q], right)

    def to_left(d, q):
        v = piece(slot(y + d, c), q)
        return remote(v, v, gls.at[d, q], glr.at[d, q], left)

    def from_right(d, q):
        v = piece(slot(y + 1 + d, c), q)
        return remote(v, v, gls.at[d, q], glr.at[d, q], left)

    def mate_copy(k, s, q):
        v = piece(s, q)
        return remote(v, v, gcs.at[k, q], gcr.at[k, q], mate)

    half = SUBS // 2
    for q in range(SUBS):
        go(to_right(0, q))
        go(to_left(0, SUBS - 1 - q))
    for q in range(SUBS):
        go(mate_copy(0, me, q))

    spot = lax.broadcasted_iota(jnp.int32, (8, 128), 0) * 128 + lax.broadcasted_iota(jnp.int32, (8, 128), 1)

    def placed(t, back):
        for j in range(NBT):
            s = slots[j, t]
            n = jnp.maximum(s - NBD, 0)
            e = (n * 43) >> 8
            b = jnp.where(s < NBD, s, NBD + e * NBND + req[n - e * CAP, e])
            places[t * NBT + j] = b
            back = jnp.where(spot == b, t * NBT + j, back)
        return back

    invv[...] = lax.fori_loop(0, TILES, placed, jnp.full((8, 128), NBD, jnp.int32))
    down = pltpu.make_async_copy(invv, inv, isem)
    down.start()
    loads[1].wait()

    def own_part(g):
        v = table[pl.ds(g * GROUP * NBT, GROUP * NBT)].reshape(GROUP * TILE, D)
        xw[at(g * GROUP, GROUP), :] = over(v, weight[:D, :], 1, 0)

    for g in range(2):
        counted(g, 0)
    chores = [functools.partial(counted, g, 0) for g in range(2, 5)]
    chores += [functools.partial(own_part, g) for g in range(4)]
    chores += [functools.partial(counted, g, 0) for g in range(5, 8)]
    for d in range(1, 5):
        for q in range(SUBS):
            if d < 4 or q < half:
                from_left(d - 1, q).wait_recv()
                if d < 3 or (d == 3 and q < half):
                    go(to_right(d, q))
                go(mate_copy(d, slot(y - d, c), q))
            b = SUBS - 1 - q
            if d < 4 or b >= half:
                from_right(d - 1, b).wait_recv()
                if d < 3 or (d == 3 and b >= half):
                    go(to_left(d, b))
                go(mate_copy(d if d == 4 else 8 - d, slot(y + d, c), b))
            if chores:
                chores.pop(0)()
    for k in range(8):
        for q in range(SUBS):
            mate_copy(k, slot(y - k, o), q).wait_recv()

    down.wait()

    def aggregated(g, _):
        cands = []
        for i in range(GROUP):
            t = g * GROUP + i
            v = jnp.concatenate([table[places[t * NBT + j]] for j in range(NBT)], axis=0)
            cand[at(t), :] = v
            cands.append(v)
        for i in range(GROUP):
            t = g * GROUP + i
            aggs[at(t), :] = (over(cn[at(t), :], cands[i], 1, 0) / DEG).astype(bf16)
        return 0

    def embedded(g, _):
        first = g * GROUP * TILE
        pre[g % 2] = xw[at(g * GROUP, GROUP), :] + over(aggs[at(g * GROUP, GROUP), :], weight[D:, :], 1, 0)
        step = 32
        for r in range(0, GROUP * TILE, step):
            v = pre[g % 2, r : r + step, :]
            gate = jax.nn.sigmoid(v)
            hid = v * gate
            scale = lax.rsqrt(jnp.mean(hid * hid, axis=-1, keepdims=True) + 1e-06)
            e = hid * scale
            where = pl.ds(first + r, step)
            emb[where, :] = e
            eh[where, :] = e.astype(bf16)
            slope[where, :] = scale * (gate * (1.0 + v * (1.0 - gate)))
        return 0

    def scored(g, loss):
        scs = [over(cand[at(g * GROUP + i), :], eh[at(g * GROUP + i), :], 1, 1) * inv_root for i in range(GROUP)]
        for i in range(GROUP):
            t = g * GROUP + i
            sc = scs[i]
            nb = nbr[:, at(t)]
            ng = neg[:, at(t)]
            ps = jnp.sum(jnp.where(nb[0:1, :] == kio, sc, 0.0), axis=0, keepdims=True)
            ns = [jnp.sum(jnp.where(ng[n : n + 1, :] == kio, sc, 0.0), axis=0, keepdims=True) for n in range(NNEG)]
            ex = 0.5 + jnp.concatenate(ns, axis=0) - ps
            loss += jax.nn.softplus(ex) * 0.25
            w = jax.nn.sigmoid(ex) * 0.25
            wn[t] = jnp.concatenate([w, jnp.sum(w, axis=0, keepdims=True), jnp.zeros((3, TILE), f32)], axis=0)
        return loss

    def backed(g, _):
        for i in range(GROUP):
            t = g * GROUP + i
            ng = neg[:, at(t)]
            v = jnp.where(nbr[0:1, at(t)] == kio, -wn[t, 4:5, :], 0.0)
            for n in range(NNEG):
                v += jnp.where(ng[n : n + 1, :] == kio, wn[t, n : n + 1, :], 0.0)
            dss[at(t), :] = (v * inv_root).astype(bf16)
        ds = [over(dss[at(g * GROUP + i), :], cand[at(g * GROUP + i), :], 0, 0) for i in range(GROUP)]
        for i in range(GROUP):
            t = g * GROUP + i
            e = emb[at(t), :]
            m2 = jnp.mean(ds[i] * e, axis=-1, keepdims=True)
            dpres[at(t), :] = (slope[at(t), :] * (ds[i] - e * m2)).astype(bf16)
        return 0

    def weighed(g):
        dp = dpres[at(g * GROUP, GROUP), :]
        for h in range(2):
            src = aggs[at(g * GROUP, GROUP), :]
            if h == 0:
                src = table[pl.ds(g * GROUP * NBT, GROUP * NBT)].reshape(GROUP * TILE, D)
            v = over(src, dp, 0, 0)
            for l in range(2):
                where = slice(l * 512 + h * 256, l * 512 + h * 256 + 256)
                part = v[:, l * 128 : l * 128 + 128]
                dw[where, :] = part if g == 0 else dw[where, :] + part

    n = TILES // GROUP
    loss = jnp.zeros((NNEG, TILE), f32)
    for step in range(n + 4):
        if step >= 4:
            weighed(step - 4)
        if 3 <= step < n + 3:
            backed(step - 3, 0)
        if 2 <= step < n + 2:
            loss = scored(step - 2, loss)
        if 1 <= step < n + 1:
            embedded(step - 1, 0)
        if step < n:
            aggregated(step, 0)
    lossp[...] = jnp.broadcast_to(jnp.sum(loss, keepdims=True), (8, 128))

    first = [
        remote(dw.at[rows(o * 512, 512), :], w0, ws.at[0, 0], wr.at[0, 0], mate),
        remote(lossp, lossb.at[0], ws.at[0, 1], wr.at[0, 1], mate),
    ]
    for copy in first:
        go(copy)

    def returned(g, _):
        di = over(dpres[at(g * GROUP, GROUP), :], weight[...], 1, 1)
        own[pl.ds(g * GROUP * NBT, GROUP * NBT)] = di[:, :D].reshape(GROUP * NBT, BLK, D)
        da = (di[:, D:] / DEG).astype(bf16)
        for i in range(GROUP):
            t = g * GROUP + i
            a = jnp.concatenate([dss[at(t), :], ct[at(t), :]], axis=1)
            b = jnp.concatenate([eh[at(t), :], da[i * TILE : (i + 1) * TILE, :]], axis=0)
            cg[pl.ds(t * NBT, NBT)] = over(a, b, 1, 0).reshape(NBT, BLK, D)
        return 0

    cg[NBD] = jnp.zeros((BLK, D), f32)

    def others(n):
        return sorted(range(1, n), key=lambda k: -min(k, n - k))

    def scatter(stage, src, base, r, buf, n, me, dev):
        buf[me] = src[rows(base + me * r, r), :]
        for k in others(n):
            to = lax.rem(me + k, n)
            go(remote(src.at[rows(base + to * r, r), :], buf.at[me], ws.at[stage, k], wr.at[stage, me], dev(k)))

    def arrived(stage, buf, n, me, dev):
        for k in range(1, n):
            who = lax.rem(me + k, n)
            remote(buf.at[who], buf.at[who], ws.at[stage, k], wr.at[stage, who], dev(k)).wait_recv()

    def spread(stage, src, buf, n, me, dev):
        buf[me] = src[...]
        for k in others(n):
            go(remote(src, buf.at[me], ws.at[stage, k], wr.at[stage, me], dev(k)))

    def summed(buf, n):
        v = buf[0]
        for i in range(1, n):
            v = v + buf[i]
        return v

    lz, lx, lossz, lossx = lossb.at[pl.ds(2, NZ)], lossb.at[pl.ds(10, NX)], lossb.at[14], lossb.at[15]

    def wa():
        for copy in first:
            copy.wait_recv()
        sum0[...] = dw[rows(c * 512, 512), :] + w0[...]
        lossb[1] = lossp[...] + lossb[0]
        scatter(1, sum0, 0, 32, a1, NZ, z, zs)
        scatter(2, sum0, 256, 64, b1, NX, x, xs)
        spread(3, lossb.at[1], lz, NZ, z, zs)

    def wb():
        arrived(2, b1, NX, x, xs)
        sum1[32:96, :] = summed(b1, NX)
        scatter(4, sum1, 32, 8, b2, NZ, z, zs)

    def wc():
        arrived(1, a1, NZ, z, zs)
        arrived(3, lz, NZ, z, zs)
        sum1[0:32, :] = summed(a1, NZ)
        lossb[14] = summed(lz, NZ)
        scatter(5, sum1, 0, 8, a2, NX, x, xs)
        spread(6, lossz, lx, NX, x, xs)

    def wd():
        arrived(4, b2, NZ, z, zs)
        arrived(5, a2, NX, x, xs)
        arrived(6, lx, NX, x, xs)
        sum2[0:8, :] = summed(a2, NX)
        sum2[8:16, :] = summed(b2, NZ)
        sum2[16:24, :] = summed(lx, NX)
        spread(7, sum2, ybuf, NY, y, ys)

    def we():
        arrived(7, ybuf, NY, y, ys)
        t = summed(ybuf, NY)
        total[...] = t
        loss_out[...] = t[16:24, :]
        spread(8, total.at[pl.ds(0, 8), :], ag2a, NX, x, xs)
        spread(9, total.at[pl.ds(8, 8), :], ag2b, NZ, z, zs)

    def wide(stage, src, r, base, n, me, dev):
        for k in others(n):
            go(remote(src, ag1.at[rows(base + me * r, r), :], ws.at[stage, k], wr.at[stage, me], dev(k)))

    def wide_arrived(stage, r, base, n, me, dev):
        for k in range(1, n):
            who = lax.rem(me + k, n)
            v = ag1.at[rows(base + who * r, r), :]
            remote(v, v, ws.at[stage, k], wr.at[stage, who], dev(k)).wait_recv()

    def wf():
        arrived(8, ag2a, NX, x, xs)
        for i in range(NX):
            sum3[i * 8 : i * 8 + 8, :] = ag2a[i]
        wide(10, sum3.at[pl.ds(0, 32), :], 32, 0, NZ, z, zs)
        ag1[rows(z * 32, 32), :] = sum3[0:32, :]

    def wg():
        arrived(9, ag2b, NZ, z, zs)
        for i in range(NZ):
            sum3[32 + i * 8 : 40 + i * 8, :] = ag2b[i]
        wide(11, sum3.at[pl.ds(32, 64), :], 64, 256, NX, x, xs)
        ag1[rows(256 + x * 64, 64), :] = sum3[32:96, :]

    last = []

    def wh():
        wide_arrived(11, 64, 256, NX, x, xs)
        last.append(go(remote(ag1.at[pl.ds(256, 256), :], dw_out.at[rows(c * 512 + 256, 256), :], ws.at[12, 1], wr.at[12, 1], mate)))
        dw_out[rows(c * 512 + 256, 256), :] = ag1[256:512, :]

    def wi():
        wide_arrived(10, 32, 0, NZ, z, zs)
        last.append(go(remote(ag1.at[pl.ds(0, 256), :], dw_out.at[rows(c * 512, 256), :], ws.at[12, 0], wr.at[12, 0], mate)))
        dw_out[rows(c * 512, 256), :] = ag1[0:256, :]


    order = [4, 3, -3, 2, -2, 1, -1, 0]

    def owner(k):
        return lax.rem(y + k + NY, NY)

    def grad_of(k, core, p):
        q = (owner(k) * 2 + core) * NBND + p
        return cg[inv[1 + q // 128, q % 128]]

    mcopies = {}

    def to_mate():
        for i, k in enumerate(order):
            for p in range(NBND):
                msend[i, p] = grad_of(k, o, p)
            mcopies[k] = go(remote(msend.at[i], mates.at[i], ms.at[i], mr.at[i], mate))

    ready = set()

    def summed_block(k, p):
        return grad_of(k, c, p) + mates[order.index(k), p]

    def wait_mate(k):
        if k not in ready:
            mcopies[k].wait_recv()
            ready.add(k)

    def hop(to_right, s, h):
        sb, rb, ss, rsm, dev = (rsend, rbuf, rs, rr, right) if to_right else (lsend, lbuf, ls, lr, left)
        view = pl.ds(h * HALF, HALF)
        return remote(sb.at[s, view], rb.at[s, view], ss.at[s, h], rsm.at[s, h], dev)

    def ring(to_right, s, h):
        start = 0 if (h == 0) == to_right else 1
        k = 4 - s if to_right else (-(4 - s) if s else 4)
        wait_mate(k)
        if s > start:
            hop(to_right, s - 1, h).wait_recv()
        for p in range(h * HALF, (h + 1) * HALF):
            v = summed_block(k, p)
            if s > start:
                v = v + (rbuf if to_right else lbuf)[s - 1, p]
            (rsend if to_right else lsend)[s, p] = v
        go(hop(to_right, s, h))

    def ringed(s, h):
        def run():
            ring(True, s, h)
            ring(False, s, 1 - h)

        return run

    def r4():
        wait_mate(0)
        for h in (1, 0):
            hop(True, 3, h).wait_recv()
            hop(False, 3, 1 - h).wait_recv()
        for p in range(NBND):
            out[p] = summed_block(0, p) + rbuf[3, p] + lbuf[3, p]

    def own_sum():
        def body(g, _):
            for i in range(8):
                b = g * 8 + i
                own[b] = own[b] + cg[inv[0, b]]
            return 0

        lax.fori_loop(0, NBD // 8, body, 0)

    lax.fori_loop(0, n // 2, returned, 0)
    wa()
    lax.fori_loop(n // 2, n, returned, 0)
    to_mate()
    for step in (
        ringed(0, 0), ringed(1, 1), wb, own_sum, wc, ringed(1, 0), wd, ringed(2, 1), ringed(2, 0), we, ringed(3, 1),
        wf, wg, ringed(3, 0), wh, wi, r4,
    ):
        step()
    for copy in last:
        copy.wait_recv()
    for copy in sent:
        copy.wait_send()


def layer(slots, req, boundary, nbr, neg, weight, features):
    vm = pl.BlockSpec(memory_space=pltpu.VMEM)
    sm = pl.BlockSpec(memory_space=pltpu.SMEM)
    hbm = pl.BlockSpec(memory_space=pl.ANY)
    V = pltpu.VMEM
    sem = pltpu.SemaphoreType.DMA
    return pl.pallas_call(
        layer_kernel,
        out_shape=(
            pltpu.VMEM((NBD, BLK, D), f32),
            pltpu.VMEM((NBND, BLK, D), f32),
            pltpu.VMEM((1024, 128), f32),
            jax.ShapeDtypeStruct((8, 128), f32),
        ),
        in_specs=[sm, sm, sm, vm, vm, vm, hbm],
        out_specs=(vm, vm, vm, vm),
        scratch_shapes=[
            V((TABLE // BLK, BLK, D), bf16),
            V((NBD, BLK, D), bf16),
            pltpu.SMEM((NBD,), jnp.int32),
            V((8, 128), jnp.int32),
            pltpu.SMEM((8, 128), jnp.int32),
            V((NODES, D), bf16),
            V((NODES, TILE), bf16),
            V((NODES, TILE), bf16),
            V((NODES, D), f32),
            V((NODES, D), bf16),
            V((NODES, D), f32),
            V((NODES, D), f32),
            V((NODES, D), bf16),
            V((NODES, TILE), bf16),
            V((TILES, 8, TILE), f32),
            V((NODES, D), bf16),
            V((NBD + 1, BLK, D), f32),
            V((2, GROUP * TILE, D), f32),
            V((8, NBND, BLK, D), f32),
            V((8, NBND, BLK, D), f32),
            V((4, NBND, BLK, D), f32),
            V((4, NBND, BLK, D), f32),
            V((4, NBND, BLK, D), f32),
            V((4, NBND, BLK, D), f32),
            V((1024, 128), f32),
            V((8, 128), f32),
            V((512, 128), f32),
            V((512, 128), f32),
            V((16, 8, 128), f32),
            V((NZ, 32, 128), f32),
            V((NX, 64, 128), f32),
            V((NX, 8, 128), f32),
            V((NZ, 8, 128), f32),
            V((96, 128), f32),
            V((96, 128), f32),
            V((24, 128), f32),
            V((NY, 24, 128), f32),
            V((24, 128), f32),
            V((NX, 8, 128), f32),
            V((NZ, 8, 128), f32),
            V((512, 128), f32),
            sem(()),
            sem(()),
            sem(()),
            sem((4, SUBS)),
            sem((4, SUBS)),
            sem((4, SUBS)),
            sem((4, SUBS)),
            sem((8, SUBS)),
            sem((8, SUBS)),
            sem((8,)),
            sem((8,)),
            sem((4, 2)),
            sem((4, 2)),
            sem((4, 2)),
            sem((4, 2)),
            sem((13, 8)),
            sem((13, 8)),
        ],
        compiler_params=pltpu.CompilerParams(collective_id=0, has_side_effects=True),
        name="layer",
    )(slots, req, boundary, nbr, neg, weight, features)


def add_kernel(boundary, lossin, got, dwt, own, out, wgrad, loss, buf, wg, sems):
    parts = 4
    n = NBD // parts
    @pl.loop(0, 16)
    def _(i):
        buf[pl.ds(i * 8, 8)] = own[pl.ds(i * 8, 8)]

    for p in range(NBND):
        b = boundary[p]
        buf[b] = buf[b] + got[p]
    outs = [pltpu.make_async_copy(buf.at[pl.ds(i * n, n)], out.at[pl.ds(i * n, n)], sems.at[i]) for i in range(parts)]
    for copy in outs:
        copy.start()
    loss[0] = lossin[0, 0] / (NODES * 512)
    wg[:, 0:128] = dwt[0:512, :] / NODES
    wg[:, 128:256] = dwt[512:1024, :] / NODES
    outs.append(pltpu.make_async_copy(wg, wgrad, sems.at[parts]))
    outs[-1].start()
    for copy in outs:
        copy.wait()


def added(boundary, lossin, got, dwt, own):
    hbm = pl.BlockSpec(memory_space=pl.ANY)
    sm = pl.BlockSpec(memory_space=pltpu.SMEM)
    vm = pl.BlockSpec(memory_space=pltpu.VMEM)
    here = [pltpu.with_memory_space_constraint(v, pltpu.VMEM) for v in (got, dwt, own)]
    return pl.pallas_call(
        add_kernel,
        out_shape=(
            jax.ShapeDtypeStruct((NBD, BLK, D), f32),
            jax.ShapeDtypeStruct((512, 256), f32),
            jax.ShapeDtypeStruct((1,), f32),
        ),
        in_specs=[sm, sm, vm, vm, vm],
        out_specs=(hbm, hbm, sm),
        scratch_shapes=[
            pltpu.VMEM((NBD, BLK, D), f32),
            pltpu.VMEM((512, 256), f32),
            pltpu.SemaphoreType.DMA((6,)),
        ],
        name="add_returned",
    )(boundary, lossin, *here)


def per_device(features, boundary, request, tile_slots, neighbors, negatives, layer_weight):
    own, got, dwt, losst = layer(
        tile_slots.T, request.T, boundary, neighbors.T, negatives.T, layer_weight, features.reshape(NBD, BLK, D)
    )
    grad, wgrad, loss = added(boundary, losst, got, dwt, own)
    return grad.reshape(NODES, D), wgrad, loss.reshape(())


def solution(mesh):
    finer = Mesh(mesh.devices.reshape(NZ, NX, NY, 2), AXES)
    dg = AXES
    return jax.shard_map(
        per_device,
        mesh=finer,
        in_specs=(P(dg, None), P(dg), P(dg, None), P(dg, None), P(dg, None), P(dg, None), P()),
        out_specs=(P(dg, None), P(), P()),
        check_vma=False,
    )
```
